32 devices in a mesh: groups: 2 (over x), ctx: 16 (over z, y, core).
Axes of the slice: x: 2, y: 2, z: 4, core: 2. Of those that a mesh axis runs over, the one named last changes fastest.
Arguments:
- pool_keys: bfloat16 [4096, 1024], P(('groups', 'ctx')), parts along dimension 0, may hold values from -6 to 6
- pool_values: bfloat16 [4096, 1024], P(('groups', 'ctx')), parts along dimension 0, may hold values from -6 to 6
- key_scales: float32 [256, 8], P(('groups', 'ctx')), parts along dimension 0, may hold values from 0.25 to 2
- value_scales: float32 [256, 8], P(('groups', 'ctx')), parts along dimension 0, may hold values from 0.25 to 2
- page_source: int32 [256], P('groups'), parts along dimension 0, may hold values from 0 to 127, as said below
- page_lengths: int32 [256], P('groups'), parts along dimension 0, may hold values from 10 to 16
- page_offsets: int32 [256], P('groups'), parts along dimension 0, may hold values from 0 to 1899, as said below
- query_positions: int32 [256], P('groups'), parts along dimension 0, may hold values from 0 to 2047
- queries: bfloat16 [256, 16384], P('groups', 'ctx'), parts along dimension 0, may hold values from -64 to 64
- out_weight: bfloat16 [16384, 16384], P('ctx'), may hold values from -0.046875 to 0.046875
Outputs:
- new_keys: bfloat16 [4096, 1024], P(('groups', 'ctx')), parts along dimension 0
- new_values: bfloat16 [4096, 1024], P(('groups', 'ctx')), parts along dimension 0
- output: bfloat16 [256, 16384], P('groups', 'ctx'), parts along dimension 0
The draws below stay inside these ranges and needn't reach their ends.
There are 2 independent parts, one for each index of `groups`. The reference program is written for one: setup_inputs(seed, part) draws one part's arguments, and reference() takes and returns one part's arrays. A program takes and returns all parts, laid end to end along the dimension named above; an argument that names none is the same for every part. Nothing has to cross between parts.
Inputs may be any that keep to these rules, and one draw needn't show every extreme that they name: `page_source`: a permutation of the pool pages; the 8 pages of one device's part of the new context come from 8 different devices, and the 8 pool pages of one device go to 8 different devices. page_offsets[0] is 0, and page_offsets[c + 1] - page_offsets[c] is page_lengths[c] plus 0 to 4.
All inputs are finite; a program needn't handle non-finite values.
Results may differ from the reference program's by a relative error of at most 0.012.
The reference program's roundings to bfloat16 on the way count: a program that leaves them out, or rounds other values in their place, can miss the bound.
Values may be sent and summed in bfloat16 or wider, within the bound.
No kernel may reach another device: no remote copies, remote signals or barrier semaphores. Data moves between devices by JAX's collectives and lax.ppermute only.
A program may use at most 128 MiB of HBM per device.

```python
import math
import jax
import jax.numpy as jnp
from jax import lax

D = 16384
H = 128
KV = 8
HD = 128
PAGE = 16
QN = 128
SLOTS = 8
NPAGES = 128


def draw_page_source(key, part):
    owners = NPAGES // SLOTS
    key_parts = jax.random.split(jax.random.fold_in(key, 11), 4)
    shifts = jax.random.permutation(key_parts[0], owners)[:SLOTS]
    relabel = jax.random.permutation(key_parts[1], owners)
    local_slot = jax.vmap(lambda item: jax.random.permutation(item, SLOTS))(jax.random.split(key_parts[2], owners))
    arrival_order = jax.vmap(lambda item: jax.random.permutation(item, SLOTS))(jax.random.split(key_parts[3], owners))
    sources = jnp.arange(owners)[:, None]
    which = jnp.arange(SLOTS)[None, :]
    owner_device = relabel[(sources + shifts[None, :]) % owners]
    position = owner_device * SLOTS + arrival_order[owner_device, which]
    source_slot = sources * SLOTS + local_slot
    source_table = jnp.zeros((NPAGES,), jnp.int32).at[position.reshape(-1)].set(source_slot.reshape(-1).astype(jnp.int32))
    return source_table.astype(jnp.int32)


def page_layout(key):
    key_parts = jax.random.split(jax.random.fold_in(key, 23), 4)
    head_count = NPAGES - 1
    length_spread = 3 * PAGE // 8 + 1
    gap_spread = PAGE // 4 + 1
    counter = jnp.arange(head_count, dtype=jnp.int32)
    head_lengths = jax.random.permutation(key_parts[0], PAGE - 3 * PAGE // 8 + counter % length_spread)
    head_gaps = jax.random.permutation(key_parts[1], counter % gap_spread)
    last_length = jax.random.randint(key_parts[2], (1,), PAGE - 3 * PAGE // 8, PAGE + 1)
    last_gap = jax.random.randint(key_parts[3], (1,), 0, PAGE // 4 + 1)
    lengths = jnp.concatenate([head_lengths, last_length]).astype(jnp.int32)
    page_gaps = jnp.concatenate([head_gaps, last_gap]).astype(jnp.int32)
    steps_total = lengths + page_gaps
    offsets = jnp.cumsum(steps_total) - steps_total
    return (lengths.astype(jnp.int32), offsets.astype(jnp.int32))


def draw_page_lengths(key, part):
    return page_layout(key)[0]


def draw_page_offsets(key, part):
    return page_layout(key)[1]


def draw_queries(key, part):
    first_key, second_key = jax.random.split(jax.random.fold_in(key, 31))
    normal_part = jnp.clip(jax.random.normal(first_key, (QN, H * HD), jnp.float32), -4.0, 4.0)
    scales = jnp.exp(jax.random.uniform(second_key, (QN, 1), jnp.float32, 0.0, math.log(2.0)))
    return (normal_part * scales).astype(jnp.bfloat16)


def set_ends(drawn, key, low, largest):
    longest = drawn.shape.index(max(drawn.shape))
    spots = []
    for shift in (0, 1):
        where = [jax.random.randint(jax.random.fold_in(key, axis), (), 0, length) for axis, length in enumerate(drawn.shape)]
        where[longest] = (where[longest] + shift) % drawn.shape[longest]
        spots.append(tuple(where))
    return drawn.at[spots[0]].set(low).at[spots[1]].set(largest)


def shard_levels(stream_key, extent, pieces, low, high):
    level, own = 1.0, jax.random.fold_in(stream_key, 6)
    for axis_at, parts in pieces:
        steps = jnp.exp(jax.random.uniform(jax.random.fold_in(own, axis_at), (parts,), jnp.float32, low / len(pieces), high / len(pieces)))
        level = level * jnp.repeat(steps, extent[axis_at] // parts).reshape([-1 if axis == axis_at else 1 for axis in range(len(extent))])
    return level


def scatter_about(rng, dims, width, bound, shards=(), kind=jnp.bfloat16):
    array = width * jax.random.normal(rng, dims, jnp.float32)
    if shards:
        array = array * shard_levels(rng, dims, shards, -0.22, 0.18)
    return jnp.clip(array, -bound, bound).astype(kind)


def setup_inputs(seed: int = 0, part: int = 0) -> dict:
    splits = jax.random.split(jax.random.key(seed), 11)
    part_splits = jax.random.split(jax.random.fold_in(splits[10], part), 11)
    return {
        "pool_keys": scatter_about(part_splits[0], (NPAGES * PAGE, KV * HD), 1.0, 6.0, ((0, 16),)),
        "pool_values": scatter_about(part_splits[1], (NPAGES * PAGE, KV * HD), 1.0, 6.0, ((0, 16),)),
        "key_scales": jnp.clip(jnp.exp(math.log(2.0) - 2.0794415 * jax.random.uniform(part_splits[2], (NPAGES, KV), jnp.float32) ** shard_levels(part_splits[2], (NPAGES, KV), ((0, 16),), -0.2, 0.2)), 0.25, 2.0),
        "value_scales": jnp.clip(jnp.exp(math.log(2.0) - 2.0794415 * jax.random.uniform(part_splits[3], (NPAGES, KV), jnp.float32) ** shard_levels(part_splits[3], (NPAGES, KV), ((0, 16),), -0.2, 0.2)), 0.25, 2.0),
        "page_source": draw_page_source(jax.random.fold_in(jax.random.fold_in(splits[10], part), 71), part),
        "page_lengths": draw_page_lengths(jax.random.fold_in(jax.random.fold_in(splits[10], part), 71), part),
        "page_offsets": draw_page_offsets(jax.random.fold_in(jax.random.fold_in(splits[10], part), 71), part),
        "query_positions": set_ends(jax.random.randint(part_splits[7], (QN,), 0, NPAGES * PAGE), jax.random.fold_in(part_splits[7], 1), 0, (NPAGES * PAGE) - 1).astype(jnp.int32),
        "queries": draw_queries(jax.random.fold_in(jax.random.fold_in(splits[10], part), 71), part),
        "out_weight": scatter_about(splits[9], (H * HD, D), (H * HD) ** -0.5, 0.046875, ((0, 16),)),
    }


rope_theta = 500000.0
scale_factor = 8.0
low_factor = 1.0
high_factor = 4.0
old_context = 8192.0
masked_score = -1.0e30


def inverse_freq():
    exponent = jnp.arange(0, HD, 2).astype(jnp.float32) / HD
    base_freq = 1.0 / (rope_theta ** exponent)
    wavelength = 2.0 * math.pi / base_freq
    smooth = (old_context / wavelength - low_factor) / (high_factor - low_factor)
    blended = (1.0 - smooth) * base_freq / scale_factor + smooth * base_freq
    short_wave = wavelength < old_context / high_factor
    longer = wavelength > old_context / low_factor
    return jnp.where(short_wave, base_freq, jnp.where(longer, base_freq / scale_factor, blended))


def rotate(values, positions):
    angle = positions.astype(jnp.float32)[:, None] * inverse_freq()[None, :]
    cosine = jnp.cos(angle)[:, None, :]
    sine_part = jnp.sin(angle)[:, None, :]
    half_size = values.shape[-1] // 2
    first_half = values[..., :half_size]
    second = values[..., half_size:]
    return jnp.concatenate([first_half * cosine - second * sine_part, second * cosine + first_half * sine_part], axis=-1)


def reference(pool_keys, pool_values, key_scales, value_scales, page_source, page_lengths, page_offsets, query_positions, queries, out_weight):
    in_page = jnp.arange(PAGE, dtype=jnp.int32)
    live_mask = in_page[None, :] < page_lengths[:, None]
    live_float = live_mask.reshape(-1).astype(jnp.float32)[:, None, None]
    slot_keys = pool_keys.reshape(NPAGES, PAGE, KV, HD).astype(jnp.float32) * key_scales[:, None, :, None]
    slot_values = pool_values.reshape(NPAGES, PAGE, KV, HD).astype(jnp.float32) * value_scales[:, None, :, None]
    moved_keys = slot_keys[page_source].reshape(NPAGES * PAGE, KV, HD)
    moved_values = slot_values[page_source].reshape(NPAGES * PAGE, KV, HD)
    page_shift = jnp.repeat(page_offsets, PAGE)
    turned = rotate(moved_keys, page_shift)
    new_keys = lax.optimization_barrier((turned * live_float).astype(jnp.bfloat16))
    new_values = lax.optimization_barrier((moved_values * live_float).astype(jnp.bfloat16))
    key_positions = (page_offsets[:, None] + in_page[None, :]).reshape(-1)
    key_live = live_mask.reshape(-1)
    turned_q = rotate(queries.astype(jnp.float32).reshape(QN, H, HD), query_positions)
    turned_q = lax.optimization_barrier(turned_q.astype(jnp.bfloat16))
    per_group = H // KV
    grouped_q = turned_q.reshape(QN, KV, per_group, HD).transpose(1, 2, 0, 3)
    keys_by_head = new_keys.transpose(1, 0, 2)
    values_by_head = new_values.transpose(1, 0, 2)
    allowed = (key_positions[None, :] <= query_positions[:, None]) & key_live[None, :]

    def one_head(operands):
        query_block, key_block, value_block = operands
        scores = jnp.einsum('gqd,kd->gqk', query_block.astype(jnp.float32), key_block.astype(jnp.float32)) * (HD ** -0.5)
        scores = jnp.where(allowed[None], scores, masked_score)
        row_max = jnp.max(scores, axis=-1, keepdims=True)
        weights = jnp.exp(scores - row_max)
        denominator = jnp.sum(weights, axis=-1)
        rounded = lax.optimization_barrier(weights.astype(jnp.bfloat16))
        summed = jnp.einsum('gqk,kd->gqd', rounded.astype(jnp.float32), value_block.astype(jnp.float32))
        return (summed / denominator[..., None]).astype(jnp.bfloat16)

    attended = lax.map(one_head, (grouped_q, keys_by_head, values_by_head))
    mixed = attended.reshape(H, QN, HD).transpose(1, 0, 2).reshape(QN, H * HD)
    output = jnp.dot(mixed, out_weight, preferred_element_type=jnp.float32).astype(jnp.bfloat16)
    return new_keys.reshape(NPAGES * PAGE, KV * HD), new_values.reshape(NPAGES * PAGE, KV * HD), output
```

```python
import math

import jax
import jax.numpy as jnp
import numpy as np
from jax import lax
from jax.experimental import pallas as pl
from jax.experimental.pallas import tpu as pltpu
from jax.sharding import PartitionSpec as P


H = 128
KV = 8
HD = 128
PAGE = 16
MIB = 1 << 20


rope_theta = 500000.0
scale_factor = 8.0
low_factor = 1.0
high_factor = 4.0
old_context = 8192.0
masked_score = -1e30
far_position = 1e9
VMEM = pl.BlockSpec(memory_space=pltpu.VMEM)
SMEM = pl.BlockSpec(memory_space=pltpu.SMEM)
HBM = pl.BlockSpec(memory_space=pltpu.HBM)
DMA = pltpu.SemaphoreType.DMA


def inverse_freq():
    exponent = np.arange(0, HD, 2).astype(np.float64) / HD
    base_freq = 1.0 / rope_theta**exponent
    wavelength = 2.0 * math.pi / base_freq
    smooth = (old_context / wavelength - low_factor) / (high_factor - low_factor)
    blended = (1.0 - smooth) * base_freq / scale_factor + smooth * base_freq
    short_wave = wavelength < old_context / high_factor
    longer = wavelength > old_context / low_factor
    return np.where(
        short_wave, base_freq, np.where(longer, base_freq / scale_factor, blended)
    ).astype(np.float32)


def lane_tables():
    freq = inverse_freq()
    sign = np.repeat([-1.0, 1.0], HD // 2)
    return jnp.asarray(np.stack([np.concatenate([freq, freq]), sign]).astype(np.float32))


def params(mib):
    return pltpu.CompilerParams(vmem_limit_bytes=mib * MIB)


def cost(flops, moved, exps=0):
    return pl.CostEstimate(flops=flops, bytes_accessed=moved, transcendentals=exps)


def shape(dims, dtype=jnp.bfloat16):
    return jax.ShapeDtypeStruct(dims, dtype)


def cos_sin(position, table_ref):
    angle = position * table_ref[0:1, :]
    return jnp.cos(angle), jnp.sin(angle) * table_ref[1:2, :]


def turn(x, cosine, sine):
    return x * cosine + pltpu.roll(x, HD // 2, 1) * sine


def column(row):
    n = row.shape[1]
    same = lax.broadcasted_iota(jnp.int32, (n, n), 0) == lax.broadcasted_iota(jnp.int32, (n, n), 1)
    return jnp.sum(jnp.where(same, row, 0.0), axis=1, keepdims=True)


def fetch(pairs, sems):
    copies = [pltpu.make_async_copy(a, b, sems.at[at]) for at, (a, b) in enumerate(pairs)]
    for copy in copies:
        copy.start()
    for copy in copies:
        copy.wait()


def in_hbm(xs):
    return [pltpu.with_memory_space_constraint(x, pltpu.HBM) for x in xs]


def vmem_like(x):
    return pltpu.VMEM(x.shape, x.dtype)


def rows_kernel(here_ref, *refs):
    inputs, out_refs, scratch, sems = refs[:8], refs[8:-9], refs[-9:-1], refs[-1]
    fetch(list(zip(inputs, scratch)), sems)
    ks_ref, vs_ref, table_ref, source_ref, lengths_ref, offsets_ref, pk_ref, pv_ref = scratch
    rows = pk_ref.shape[0]
    slots = rows // PAGE
    pages = source_ref.shape[1]
    row = lax.broadcasted_iota(jnp.int32, (rows, pages), 0)
    match = source_ref[...] == here_ref[0] * slots + row // PAGE

    def pick(ref):
        return jnp.sum(jnp.where(match, ref[...].astype(jnp.float32), 0.0), axis=1, keepdims=True)

    position, length = pick(offsets_ref), pick(lengths_ref)
    cosine, sine = cos_sin(position, table_ref)
    token = (lax.broadcasted_iota(jnp.int32, (rows, 1), 0) % PAGE).astype(jnp.float32)
    live = jnp.broadcast_to((token < length).astype(jnp.float32), (rows, HD))
    for piece, out_ref in enumerate(out_refs):
        head = jnp.bitwise_xor(here_ref[0] // 2, piece)
        lanes = pl.ds(pl.multiple_of(head * HD, HD), HD)
        for slot in range(slots):
            part = slice(slot * PAGE, (slot + 1) * PAGE)
            k = pk_ref[part, lanes].astype(jnp.float32) * ks_ref[slot, head]
            k = turn(k, cosine[part], sine[part]) * live[part]
            out_ref[0, part, :] = k.astype(jnp.bfloat16)
            v = pv_ref[part, lanes].astype(jnp.float32) * vs_ref[slot, head]
            out_ref[1, part, :] = (v * live[part]).astype(jnp.bfloat16)


def prepare_rows(here, pool_keys, pool_values, key_scales, value_scales, source, lengths, offsets):
    rows = pool_keys.shape[0]
    table = lane_tables()
    small = [pltpu.SMEM(key_scales.shape, jnp.float32)] * 2
    inputs = (key_scales, value_scales, table, source, lengths, offsets, pool_keys, pool_values)
    return pl.pallas_call(
        rows_kernel,
        out_shape=[shape((2, rows, HD))] * KV,
        in_specs=[SMEM] + [HBM] * 8,
        out_specs=[VMEM] * KV,
        scratch_shapes=small + [vmem_like(x) for x in inputs[2:]] + [DMA((8,))],
        name="prepare_rows",
        compiler_params=params(6),
        cost_estimate=cost(20 * rows * KV * HD, 8 * rows * KV * HD),
    )(here, *in_hbm(inputs))


def side_kernel(here_ref, *refs):
    inputs, (out_ref, kpos_ref), scratch, sems = refs[:6], refs[6:8], refs[8:14], refs[14]
    fetch(list(zip(inputs, scratch)), sems)
    table_ref, source_ref, lengths_ref, offsets_ref, position_ref, q_ref = scratch
    count = q_ref.shape[0]
    cosine, sine = cos_sin(column(position_ref[...].astype(jnp.float32)), table_ref)
    for head in range(q_ref.shape[1] // HD):
        q = q_ref[:, head * HD : (head + 1) * HD].astype(jnp.float32)
        out_ref[head * count : (head + 1) * count, :] = turn(q, cosine, sine).astype(jnp.bfloat16)
    source = column(source_ref[...].astype(jnp.float32))
    length = column(lengths_ref[...].astype(jnp.float32))
    offset = column(offsets_ref[...].astype(jnp.float32))
    tokens = kpos_ref.shape[1]
    rows = tokens // (2 * KV)
    slots = rows // PAGE
    at = lax.broadcasted_iota(jnp.int32, (1, rows), 1)
    token = (at % PAGE).astype(jnp.float32)
    where = jnp.where(token < length, offset + token, far_position)
    for group in range(2 * KV):
        half, piece = group // KV, group % KV
        device = jnp.bitwise_xor(here_ref[0], 2 * piece + half)
        page = (device * slots + at // PAGE).astype(jnp.float32)
        kpos_ref[:, group * rows : (group + 1) * rows] = jnp.sum(
            jnp.where(source == page, where, 0.0), axis=0, keepdims=True
        )


def side(here, source, lengths, offsets, positions, queries):
    count, width = queries.shape
    tokens = source.shape[1] * PAGE
    inputs = (lane_tables(), source, lengths, offsets, positions, queries)
    return pl.pallas_call(
        side_kernel,
        out_shape=(shape((count * (width // HD), HD)), shape((1, tokens), jnp.float32)),
        in_specs=[SMEM] + [HBM] * 6,
        out_specs=(VMEM, VMEM),
        scratch_shapes=[vmem_like(x) for x in inputs] + [DMA((6,))],
        name="side",
        compiler_params=params(6),
        cost_estimate=cost(8 * count * width, 64 * MIB),
    )(here, *in_hbm(inputs))


def assemble_kernel(*refs):
    for at, ref in enumerate(refs[:-1]):
        refs[-1][at] = ref[...]


def assemble(pieces):
    dims = (len(pieces), *pieces[0].shape)
    return pl.pallas_call(
        assemble_kernel,
        out_shape=shape(dims),
        in_specs=[VMEM] * len(pieces),
        out_specs=VMEM,
        compiler_params=params(2),
        cost_estimate=cost(0, 4 * math.prod(dims)),
    )(*pieces)


def pages_kernel(here_ref, source_ref, *refs):
    context, out_refs, page_ref, place_ref = refs[: -KV - 2], refs[-KV - 2 : -2], refs[-2], refs[-1]
    pages = source_ref.shape[0]
    slots = pages // (2 * KV)
    here = here_ref[0]
    kind = here % 2
    for page in range(pages):
        place_ref[source_ref[page]] = page
    group = 0
    for ref in context:
        for at in range(ref.shape[0]):
            half, piece = group // KV, group % KV
            device = jnp.bitwise_xor(here, 2 * piece + half)
            for slot in range(slots):
                page = place_ref[device * slots + slot]
                page_ref[page] = ref[at, kind, slot * PAGE : (slot + 1) * PAGE, :]
            group += 1
    for piece, out_ref in enumerate(out_refs):
        first = jnp.bitwise_xor(here // 2, piece) * 2 * slots
        out_ref[...] = page_ref[pl.ds(first, 2 * slots)]


def order_pages(here, source, context):
    pages = source.shape[0]
    return pl.pallas_call(
        pages_kernel,
        out_shape=[shape((pages // KV, PAGE, HD))] * KV,
        in_specs=[SMEM, SMEM] + [VMEM] * len(context),
        out_specs=[VMEM] * KV,
        scratch_shapes=[pltpu.VMEM((pages, PAGE, HD), jnp.bfloat16), pltpu.SMEM((pages,), jnp.int32)],
        name="order_pages",
        compiler_params=params(4),
        cost_estimate=cost(0, 4 * pages * PAGE * HD),
    )(here, source, *context)


def collect_kernel(here_ref, *refs):
    pieces, (keep_ref, send_ref) = refs[:-2], refs[-2:]
    rows = keep_ref.shape[0]
    slots = rows // PAGE
    core = here_ref[0] % 2
    for piece, ref in enumerate(pieces):
        head = jnp.bitwise_xor(here_ref[0] // 2, piece)
        lanes = pl.ds(pl.multiple_of(head * HD, HD), HD)
        keep_ref[:, lanes] = ref[pl.ds(core * slots, slots)].reshape(rows, HD)
        send_ref[:, lanes] = ref[pl.ds((1 - core) * slots, slots)].reshape(rows, HD)


def collect_heads(here, pieces):
    rows = pieces[0].shape[0] * PAGE // 2
    out = shape((rows, KV * HD))
    return pl.pallas_call(
        collect_kernel,
        out_shape=(out, out),
        in_specs=[SMEM] + [VMEM] * KV,
        out_specs=(VMEM, VMEM),
        name="collect_heads",
        compiler_params=params(4),
        cost_estimate=cost(0, 8 * rows * KV * HD),
    )(here, *pieces)


def settle_kernel(here_ref, mine_ref, other_ref, keys_ref, values_ref):
    first = here_ref[0] % 2 == 0
    keys_ref[...] = jnp.where(first, mine_ref[...], other_ref[...])
    values_ref[...] = jnp.where(first, other_ref[...], mine_ref[...])


def settle(here, mine, other):
    return pl.pallas_call(
        settle_kernel,
        out_shape=(shape(mine.shape), shape(mine.shape)),
        in_specs=[SMEM, VMEM, VMEM],
        out_specs=(VMEM, VMEM),
        name="settle",
        compiler_params=params(4),
        cost_estimate=cost(0, 8 * math.prod(mine.shape)),
    )(here, mine, other)


def attention_kernel(*refs):
    context, (q_ref, kpos_ref, qpos_ref, out_ref, s_ref) = refs[:-5], refs[-5:]
    count = qpos_ref.shape[1]
    heads = q_ref.shape[0] // count
    rows = context[0].shape[2]
    blocks, at = [], 0
    for ref in context:
        step = max(1, min(ref.shape[0], 512 // rows))
        for first in range(0, ref.shape[0], step):
            blocks.append((ref, slice(first, first + step), slice(at, at + step * rows)))
            at += step * rows
    block = step * rows
    scale = HD**-0.5 * math.log2(math.e)
    qpos = column(qpos_ref[...].astype(jnp.float32))

    def one(head, carry):
        q = q_ref[pl.ds(pl.multiple_of(head * count, count), count), :]
        top = jnp.full((count, HD), masked_score, jnp.float32)
        for ref, chips, lanes in blocks:
            s = lax.dot_general(
                q,
                ref[chips, 0].reshape(block, HD),
                (((1,), (1,)), ((), ())),
                preferred_element_type=jnp.float32,
            )
            s = jnp.where(kpos_ref[:, lanes] <= qpos, s, masked_score)
            s_ref[:, lanes] = s
            for lane in range(0, block, HD):
                top = jnp.maximum(top, s[:, lane : lane + HD])
        top = jnp.max(top, axis=1, keepdims=True)
        total = jnp.zeros((count, HD), jnp.float32)
        summed = jnp.zeros((count, HD), jnp.float32)
        for ref, chips, lanes in blocks:
            w = jnp.exp2((s_ref[:, lanes] - top) * scale)
            for lane in range(0, block, HD):
                total = total + w[:, lane : lane + HD]
            summed = summed + jnp.dot(
                w.astype(jnp.bfloat16),
                ref[chips, 1].reshape(block, HD),
                preferred_element_type=jnp.float32,
            )
        total = jnp.sum(total, axis=1, keepdims=True)
        out_ref[:, pl.ds(pl.multiple_of(head * HD, HD), HD)] = (summed / total).astype(jnp.bfloat16)
        return carry

    lax.fori_loop(0, heads, one, 0)


def attend(context, q, key_positions, query_positions):
    tokens = key_positions.shape[1]
    count = query_positions.shape[1]
    heads = q.shape[0] // count
    return pl.pallas_call(
        attention_kernel,
        out_shape=shape((count, heads * HD)),
        in_specs=[VMEM] * (len(context) + 3),
        out_specs=VMEM,
        scratch_shapes=[pltpu.VMEM((count, tokens), jnp.float32)],
        name="attend",
        compiler_params=params(6),
        cost_estimate=cost(
            4 * count * heads * tokens * HD, 4 * tokens * HD, count * heads * tokens
        ),
    )(*context, q, key_positions, query_positions)


def fold_masks(bits):
    masks = [0]
    for bit in reversed(bits):
        masks = masks + [m | bit for m in masks]
    return masks


def columns_of(here_ref, mask, width, start, w_ref):
    own_width = w_ref.shape[1] // (2 * KV)
    first = jnp.bitwise_xor(here_ref[0], mask) * own_width + start
    return pl.ds(pl.multiple_of(first, HD), width)


def project_send_kernel(masks, start, here_ref, x_ref, w_ref, out_ref):
    for at, mask in enumerate(masks):
        columns = columns_of(here_ref, mask, out_ref.shape[2], start, w_ref)
        out_ref[at] = jnp.dot(
            x_ref[...], w_ref[:, columns], preferred_element_type=jnp.float32
        ).astype(jnp.bfloat16)


def project_keep_kernel(masks, start, here_ref, x_ref, w_ref, got_ref, send_ref, keep_ref):
    half = len(masks) // 2
    for at in list(range(half, 2 * half)) + list(range(half)):
        columns = columns_of(here_ref, masks[at], got_ref.shape[2], start, w_ref)
        y = jnp.dot(x_ref[...], w_ref[:, columns], preferred_element_type=jnp.float32)
        y = y + got_ref[at].astype(jnp.float32)
        if at >= half:
            send_ref[at - half] = y.astype(jnp.bfloat16)
        else:
            keep_ref[at] = y


def project_cost(x, w, columns):
    return cost(2 * x.shape[0] * w.shape[0] * columns, 2 * w.shape[0] * columns)


def project_send(here, mixed, weight, masks, start, width):
    count = mixed.shape[0]
    return pl.pallas_call(
        lambda *refs: project_send_kernel(masks, start, *refs),
        out_shape=shape((len(masks), count, width)),
        in_specs=[SMEM, VMEM, VMEM],
        out_specs=VMEM,
        compiler_params=params(6),
        cost_estimate=project_cost(mixed, weight, len(masks) * width),
    )(here, mixed, weight)


def project_keep(here, mixed, weight, got, masks, start):
    count = mixed.shape[0]
    half, width = len(masks) // 2, got.shape[2]
    return pl.pallas_call(
        lambda *refs: project_keep_kernel(masks, start, *refs),
        out_shape=(shape((half, count, width)), shape((half, count, width), jnp.float32)),
        in_specs=[SMEM, VMEM, VMEM, VMEM],
        out_specs=(VMEM, VMEM),
        compiler_params=params(6),
        cost_estimate=project_cost(mixed, weight, len(masks) * width),
    )(here, mixed, weight, got)


def fold_kernel(keep_ref, got_ref, send_ref, left_ref):
    left = left_ref.shape[0]
    for at in range(left):
        send_ref[at] = (keep_ref[left + at] + got_ref[left + at].astype(jnp.float32)).astype(
            jnp.bfloat16
        )
    for at in range(left):
        left_ref[at] = keep_ref[at] + got_ref[at].astype(jnp.float32)


def fold(keep, got):
    owners, count, width = keep.shape
    half = (owners // 2, count, width)
    return pl.pallas_call(
        fold_kernel,
        out_shape=(shape(half), shape(half, jnp.float32)),
        in_specs=[VMEM, VMEM],
        out_specs=(VMEM, VMEM),
        compiler_params=params(4),
        cost_estimate=cost(owners * count * width, 8 * owners * count * width),
    )(keep, got)


def finish_kernel(*refs):
    out_ref, at = refs[-1], 0
    for keep_ref, got_ref in zip(refs[:-1:2], refs[1:-1:2]):
        width = keep_ref.shape[2]
        total = keep_ref[0] + got_ref[0].astype(jnp.float32)
        out_ref[:, at : at + width] = total.astype(jnp.bfloat16)
        at += width


def finish(pairs):
    flat = [x for pair in pairs for x in pair]
    count = flat[0].shape[1]
    width = sum(keep.shape[2] for keep, _ in pairs)
    return pl.pallas_call(
        finish_kernel,
        out_shape=shape((count, width)),
        in_specs=[VMEM] * len(flat),
        out_specs=VMEM,
        name="finish",
        compiler_params=params(4),
        cost_estimate=cost(count * width, 8 * count * width),
    )(*flat)


def swap(x, bits, devices):
    return lax.ppermute(x, "ctx", [(d, d ^ bits) for d in range(devices)])


def after(x, *others):
    return lax.optimization_barrier((x, *others))[0]


def plan(devices, own_width):
    bits = [1 << b for b in range(devices.bit_length() - 1)]
    half = own_width // 2
    return [
        (0, half, bits),
        (half, half, [bits[0], bits[2], bits[1]] + bits[3:]),
    ]


def project_and_scatter(here, devices, x, weight, chunks):
    masks = [fold_masks(order) for _, _, order in chunks]
    half = devices // 2
    state, got = [], []
    for at, (start, width, order) in enumerate(chunks):
        out = project_send(here, x, weight, masks[at][half:], start, width)
        got.append(swap(out, order[0], devices))
        x = after(x, out)
    for at, (start, _, _) in enumerate(chunks):
        send, keep = project_keep(here, x, weight, got[at], masks[at][:half], start)
        state.append((send, keep))
        x = after(x, send)
    stages = len(chunks[0][2])
    for stage in range(1, stages):
        arrived = [swap(send, chunks[at][2][stage], devices) for at, (send, _) in enumerate(state)]
        if stage + 1 < stages:
            state = [fold(keep, got) for (_, keep), got in zip(state, arrived)]
    return finish([(keep, got) for (_, keep), got in zip(state, arrived)])


def body(
    pool_keys,
    pool_values,
    key_scales,
    value_scales,
    page_source,
    page_lengths,
    page_offsets,
    query_positions,
    queries,
    out_weight,
):
    devices = lax.axis_size("ctx")
    here = lax.axis_index("ctx").astype(jnp.int32)[None]
    source, lengths, offsets = page_source[None], page_lengths[None], page_offsets[None]
    positions = query_positions[None]
    pieces = prepare_rows(
        here, pool_keys, pool_values, key_scales, value_scales, source, lengths, offsets
    )
    far = range(KV // 2, KV)
    arrived = [pieces[0]] + [swap(pieces[k], 2 * k, devices) for k in range(1, KV)]
    turned, key_positions = side(here, source, lengths, offsets, positions, queries)
    chunks = plan(devices, out_weight.shape[1] // devices)
    near = assemble(arrived[: KV // 2])
    far = assemble(arrived[KV // 2 :])
    context = [near, far, swap(near, 1, devices), swap(far, 1, devices)]
    leaving = order_pages(here, page_source, context)
    pages = [leaving[0]] + [swap(leaving[k], 2 * k, devices) for k in range(1, KV)]
    mixed = attend(context, turned, key_positions, positions)
    output = project_and_scatter(here, devices, mixed, out_weight, chunks)
    mine, partner = collect_heads(here, pages)
    new_keys, new_values = settle(here, mine, swap(partner, 1, devices))
    return (new_keys, new_values, output)


def wide_inverse_freq():
    exponent = jnp.arange(0, HD, 2).astype(jnp.float32) / HD
    base_freq = 1.0 / rope_theta**exponent
    wavelength = 2.0 * math.pi / base_freq
    smooth = (old_context / wavelength - low_factor) / (high_factor - low_factor)
    blended = (1.0 - smooth) * base_freq / scale_factor + smooth * base_freq
    short_wave = wavelength < old_context / high_factor
    longer = wavelength > old_context / low_factor
    return jnp.where(short_wave, base_freq, jnp.where(longer, base_freq / scale_factor, blended))


def rotate(values, positions):
    angle = positions.astype(jnp.float32)[:, None] * wide_inverse_freq()[None, :]
    cosine = jnp.cos(angle)[:, None, :]
    sine_part = jnp.sin(angle)[:, None, :]
    half_size = values.shape[-1] // 2
    first_half = values[..., :half_size]
    second = values[..., half_size:]
    return jnp.concatenate(
        [first_half * cosine - second * sine_part, second * cosine + first_half * sine_part],
        axis=-1,
    )


def wide_body(
    pool_keys,
    pool_values,
    key_scales,
    value_scales,
    page_source,
    page_lengths,
    page_offsets,
    query_positions,
    queries,
    out_weight,
):
    devices = lax.axis_size("ctx")
    here_index = lax.axis_index("ctx")
    slot_count = key_scales.shape[0]
    page_count = page_source.shape[0]
    query_count = queries.shape[0]
    local_heads = queries.shape[1] // HD
    per_group = H // KV
    in_page = jnp.arange(PAGE, dtype=jnp.int32)
    inverse = (
        jnp.zeros((page_count,), jnp.int32)
        .at[page_source]
        .set(jnp.arange(page_count, dtype=jnp.int32))
    )
    held_pages = lax.dynamic_slice_in_dim(inverse, here_index * slot_count, slot_count)
    held_live = in_page[None, :] < page_lengths[held_pages][:, None]
    live_float = held_live.reshape(-1).astype(jnp.float32)[:, None, None]
    scaled_keys = (
        pool_keys.reshape(slot_count, PAGE, KV, HD).astype(jnp.float32)
        * key_scales[:, None, :, None]
    )
    scaled_values = (
        pool_values.reshape(slot_count, PAGE, KV, HD).astype(jnp.float32)
        * value_scales[:, None, :, None]
    )
    turned = rotate(
        scaled_keys.reshape(slot_count * PAGE, KV, HD), jnp.repeat(page_offsets[held_pages], PAGE)
    )
    slot_keys = (turned * live_float).astype(jnp.bfloat16).reshape(slot_count, PAGE * KV * HD)
    slot_values = (
        (scaled_values.reshape(slot_count * PAGE, KV, HD) * live_float)
        .astype(jnp.bfloat16)
        .reshape(slot_count, PAGE * KV * HD)
    )
    owner_device = held_pages // slot_count
    routing = (owner_device[None, :] == jnp.arange(devices, dtype=jnp.int32)[:, None]).astype(
        jnp.bfloat16
    )
    outgoing_keys = jnp.dot(routing, slot_keys, preferred_element_type=jnp.float32).astype(
        jnp.bfloat16
    )
    outgoing_values = jnp.dot(routing, slot_values, preferred_element_type=jnp.float32).astype(
        jnp.bfloat16
    )
    arrived_keys, arrived_values = (
        lax.all_to_all(outgoing_keys, "ctx", split_axis=0, concat_axis=0, tiled=True),
        lax.all_to_all(outgoing_values, "ctx", split_axis=0, concat_axis=0, tiled=True),
    )
    assembled_pages = here_index * slot_count + jnp.arange(slot_count, dtype=jnp.int32)
    sender = page_source[assembled_pages] // slot_count
    new_keys = arrived_keys[sender].reshape(slot_count * PAGE, KV * HD)
    new_values = arrived_values[sender].reshape(slot_count * PAGE, KV * HD)
    local_keys = slot_keys.reshape(slot_count * PAGE, KV * HD)
    local_values = slot_values.reshape(slot_count * PAGE, KV * HD)
    local_tokens = local_keys.shape[0]
    turned_q = rotate(
        queries.astype(jnp.float32).reshape(query_count, local_heads, HD), query_positions
    )
    own_queries = turned_q.astype(jnp.bfloat16).transpose(1, 0, 2)
    target = jnp.arange(devices, dtype=jnp.int32) * local_heads // per_group
    keys_by_head = local_keys.reshape(local_tokens, KV, HD).transpose(1, 0, 2)
    values_by_head = local_values.reshape(local_tokens, KV, HD).transpose(1, 0, 2)
    head_keys, head_values = (
        lax.all_to_all(keys_by_head[target], "ctx", split_axis=0, concat_axis=0, tiled=True),
        lax.all_to_all(values_by_head[target], "ctx", split_axis=0, concat_axis=0, tiled=True),
    )
    key_positions = (page_offsets[inverse][:, None] + in_page[None, :]).reshape(-1)
    key_live = (in_page[None, :] < page_lengths[inverse][:, None]).reshape(-1)
    key_positions, key_live = (key_positions, key_live)
    allowed = (key_positions[None, :] <= query_positions[:, None]) & key_live[None, :]
    span_devices = max(1, min(devices, 4096 // local_tokens))
    while span_devices > 1 and devices % span_devices:
        span_devices -= 1
    block_count = devices // span_devices
    key_blocks = head_keys.reshape(block_count, span_devices * local_tokens, HD)
    value_blocks = head_values.reshape(block_count, span_devices * local_tokens, HD)
    allowed_blocks = allowed.reshape(
        query_count, block_count, span_devices * local_tokens
    ).transpose(1, 0, 2)

    def block_scores(key_block, allow_block):
        scores = jnp.einsum(
            "hqd,kd->hqk", own_queries, key_block, preferred_element_type=jnp.float32
        ) * HD ** (-0.5)
        return jnp.where(allow_block[None], scores, masked_score)

    block_max = lax.map(
        lambda operands: jnp.max(block_scores(operands[0], operands[1]), axis=-1),
        (key_blocks, allowed_blocks),
    )
    row_max = jnp.max(block_max, axis=0)

    def weigh_block(operands):
        key_block, value_block, allow_block = operands
        weights = jnp.exp(block_scores(key_block, allow_block) - row_max[..., None])
        denominator = jnp.sum(weights, axis=-1)
        summed = jnp.einsum(
            "hqk,kd->hqd",
            weights.astype(jnp.bfloat16),
            value_block,
            preferred_element_type=jnp.float32,
        )
        return (summed, denominator)

    summed, denominator = lax.map(weigh_block, (key_blocks, value_blocks, allowed_blocks))
    summed = jnp.sum(summed, axis=0)
    denominator = jnp.sum(denominator, axis=0)
    attended = (summed / denominator[..., None]).astype(jnp.bfloat16)
    mixed = attended.transpose(1, 0, 2).reshape(query_count, local_heads * HD)
    reduced = lax.psum_scatter(
        lax.dot_general(
            out_weight, mixed, (((0,), (1,)), ((), ())), preferred_element_type=jnp.float32
        ),
        "ctx",
        scatter_dimension=0,
        tiled=True,
    )
    output = reduced.T.astype(jnp.bfloat16)
    return (new_keys, new_values, output)


def solution(mesh):
    in_specs = (
        P(("groups", "ctx"), None),
        P(("groups", "ctx"), None),
        P(("groups", "ctx"), None),
        P(("groups", "ctx"), None),
        P("groups"),
        P("groups"),
        P("groups"),
        P("groups"),
        P("groups", "ctx"),
        P("ctx", None),
    )
    out_specs = (P(("groups", "ctx"), None), P(("groups", "ctx"), None), P("groups", "ctx"))
    fits = mesh.shape["ctx"] == 2 * KV
    chosen = body if fits else wide_body
    return jax.shard_map(
        chosen, mesh=mesh, in_specs=in_specs, out_specs=out_specs, check_vma=False
    )
```

```python
import math

import jax
import jax.numpy as jnp
import numpy as np
from jax import lax
from jax.experimental import pallas as pl
from jax.experimental.pallas import tpu as pltpu
from jax.sharding import PartitionSpec as P


H = 128
KV = 8
HD = 128
PAGE = 16
MIB = 1 << 20
UNROLL = 1
EARLY = 12


rope_theta = 500000.0
scale_factor = 8.0
low_factor = 1.0
high_factor = 4.0
old_context = 8192.0
masked_score = -1e30
far_position = 1e9
VMEM = pl.BlockSpec(memory_space=pltpu.VMEM)
SMEM = pl.BlockSpec(memory_space=pltpu.SMEM)
HBM = pl.BlockSpec(memory_space=pltpu.HBM)
DMA = pltpu.SemaphoreType.DMA


def inverse_freq():
    exponent = np.arange(0, HD, 2).astype(np.float64) / HD
    base_freq = 1.0 / rope_theta**exponent
    wavelength = 2.0 * math.pi / base_freq
    smooth = (old_context / wavelength - low_factor) / (high_factor - low_factor)
    blended = (1.0 - smooth) * base_freq / scale_factor + smooth * base_freq
    short_wave = wavelength < old_context / high_factor
    longer = wavelength > old_context / low_factor
    return np.where(
        short_wave, base_freq, np.where(longer, base_freq / scale_factor, blended)
    ).astype(np.float32)


def lane_tables():
    freq = inverse_freq()
    sign = np.repeat([-1.0, 1.0], HD // 2)
    return jnp.asarray(np.stack([np.concatenate([freq, freq]), sign]).astype(np.float32))


def params(mib):
    return pltpu.CompilerParams(vmem_limit_bytes=mib * MIB)


def cost(flops, moved, exps=0):
    return pl.CostEstimate(flops=flops, bytes_accessed=moved, transcendentals=exps)


def shape(dims, dtype=jnp.bfloat16):
    return jax.ShapeDtypeStruct(dims, dtype)


def cos_sin(position, table_ref):
    angle = position * table_ref[0:1, :]
    return jnp.cos(angle), jnp.sin(angle) * table_ref[1:2, :]


def turn(x, cosine, sine):
    return x * cosine + pltpu.roll(x, HD // 2, 1) * sine


def column(row):
    n = row.shape[1]
    same = lax.broadcasted_iota(jnp.int32, (n, n), 0) == lax.broadcasted_iota(jnp.int32, (n, n), 1)
    return jnp.sum(jnp.where(same, row, 0.0), axis=1, keepdims=True)


def fetch(pairs, sems, meanwhile=None):
    copies = [pltpu.make_async_copy(a, b, sems.at[at]) for at, (a, b) in enumerate(pairs)]
    for copy in copies:
        copy.start()
    if meanwhile is not None:
        meanwhile()
    for copy in copies:
        copy.wait()


def in_hbm(xs):
    return [pltpu.with_memory_space_constraint(x, pltpu.HBM) for x in xs]


def vmem_like(x):
    return pltpu.VMEM(x.shape, x.dtype)


def rows_kernel(here_ref, *refs):
    inputs, out_refs, scratch, sems = refs[:8], refs[8:-9], refs[-9:-1], refs[-1]
    fetch(list(zip(inputs, scratch)), sems)
    ks_ref, vs_ref, table_ref, source_ref, lengths_ref, offsets_ref, pk_ref, pv_ref = scratch
    rows = pk_ref.shape[0]
    slots = rows // PAGE
    pages = source_ref.shape[1]
    row = lax.broadcasted_iota(jnp.int32, (rows, pages), 0)
    match = source_ref[...] == here_ref[0] * slots + row // PAGE

    def pick(ref):
        return jnp.sum(jnp.where(match, ref[...].astype(jnp.float32), 0.0), axis=1, keepdims=True)

    position, length = pick(offsets_ref), pick(lengths_ref)
    cosine, sine = cos_sin(position, table_ref)
    token = (lax.broadcasted_iota(jnp.int32, (rows, 1), 0) % PAGE).astype(jnp.float32)
    live = jnp.broadcast_to((token < length).astype(jnp.float32), (rows, HD))
    for piece, out_ref in enumerate(out_refs):
        head = jnp.bitwise_xor(here_ref[0] // 2, piece)
        lanes = pl.ds(pl.multiple_of(head * HD, HD), HD)
        for slot in range(slots):
            part = slice(slot * PAGE, (slot + 1) * PAGE)
            k = pk_ref[part, lanes].astype(jnp.float32) * ks_ref[slot, head]
            k = turn(k, cosine[part], sine[part]) * live[part]
            out_ref[0, part, :] = k.astype(jnp.bfloat16)
            v = pv_ref[part, lanes].astype(jnp.float32) * vs_ref[slot, head]
            out_ref[1, part, :] = (v * live[part]).astype(jnp.bfloat16)


def prepare_rows(here, pool_keys, pool_values, key_scales, value_scales, source, lengths, offsets):
    rows = pool_keys.shape[0]
    table = lane_tables()
    small = [pltpu.SMEM(key_scales.shape, jnp.float32)] * 2
    inputs = (key_scales, value_scales, table, source, lengths, offsets, pool_keys, pool_values)
    return pl.pallas_call(
        rows_kernel,
        out_shape=[shape((2, rows, HD))] * KV,
        in_specs=[SMEM] + [HBM] * 8,
        out_specs=[VMEM] * KV,
        scratch_shapes=small + [vmem_like(x) for x in inputs[2:]] + [DMA((8,))],
        name="prepare_rows",
        compiler_params=params(6),
        cost_estimate=cost(20 * rows * KV * HD, 8 * rows * KV * HD),
    )(here, *in_hbm(inputs))


def weight_parts(w_ref, pieces, refs, owners):
    own_width = w_ref.shape[1] // owners
    parts = []
    for (first, last, start, width), ref in zip(pieces, refs):
        for owner in range(owners):
            columns = pl.ds(owner * own_width + start, width)
            parts.append(
                (w_ref.at[first:last, columns], ref.at[:, pl.ds(owner * width, width)])
            )
    return parts


def weight_shapes(pieces, owners):
    return [shape((last - first, owners * width)) for first, last, _, width in pieces]


def side_kernel(pieces, owners, here_ref, w_ref, *refs):
    inputs, outs, refs = refs[:6], refs[6:8], refs[8:]
    held, scratch, sems, weight_sems = refs[: len(pieces)], refs[len(pieces) : -2], refs[-2], refs[-1]

    def compute():
        fetch(list(zip(inputs, scratch)), sems)
        side_rows(here_ref, *scratch, *outs)

    fetch(weight_parts(w_ref, pieces, held, owners), weight_sems, compute)


def side_rows(here_ref, *refs):
    (out_ref, kpos_ref), scratch = refs[-2:], refs[:-2]
    table_ref, source_ref, lengths_ref, offsets_ref, position_ref, q_ref = scratch
    count = q_ref.shape[0]
    cosine, sine = cos_sin(column(position_ref[...].astype(jnp.float32)), table_ref)
    for head in range(q_ref.shape[1] // HD):
        q = q_ref[:, head * HD : (head + 1) * HD].astype(jnp.float32)
        out_ref[head * count : (head + 1) * count, :] = turn(q, cosine, sine).astype(jnp.bfloat16)
    source = column(source_ref[...].astype(jnp.float32))
    length = column(lengths_ref[...].astype(jnp.float32))
    offset = column(offsets_ref[...].astype(jnp.float32))
    tokens = kpos_ref.shape[1]
    rows = tokens // (2 * KV)
    slots = rows // PAGE
    at = lax.broadcasted_iota(jnp.int32, (1, rows), 1)
    token = (at % PAGE).astype(jnp.float32)
    where = jnp.where(token < length, offset + token, far_position)
    for group in range(2 * KV):
        half, piece = group // KV, group % KV
        device = jnp.bitwise_xor(here_ref[0], 2 * piece + half)
        page = (device * slots + at // PAGE).astype(jnp.float32)
        kpos_ref[:, group * rows : (group + 1) * rows] = jnp.sum(
            jnp.where(source == page, where, 0.0), axis=0, keepdims=True
        )


def side(here, source, lengths, offsets, positions, queries, out_weight, pieces, owners):
    count, width = queries.shape
    tokens = source.shape[1] * PAGE
    inputs = (lane_tables(), source, lengths, offsets, positions, queries)
    outs = [shape((count * (width // HD), HD)), shape((1, tokens), jnp.float32)]
    outs += weight_shapes(pieces, owners)
    return pl.pallas_call(
        lambda *refs: side_kernel(pieces, owners, *refs),
        out_shape=outs,
        in_specs=[SMEM] + [HBM] * 7,
        out_specs=[VMEM] * len(outs),
        scratch_shapes=[vmem_like(x) for x in inputs] + [DMA((6,)), DMA((len(pieces) * owners,))],
        name="side",
        compiler_params=params(6),
        cost_estimate=cost(8 * count * width, 64 * MIB),
    )(here, *in_hbm((out_weight, *inputs)))


def assemble_kernel(*refs):
    for at, ref in enumerate(refs[:-1]):
        refs[-1][at] = ref[...]


def assemble(pieces):
    dims = (len(pieces), *pieces[0].shape)
    return pl.pallas_call(
        assemble_kernel,
        out_shape=shape(dims),
        in_specs=[VMEM] * len(pieces),
        out_specs=VMEM,
        compiler_params=params(2),
        cost_estimate=cost(0, 4 * math.prod(dims)),
    )(*pieces)


def pages_kernel(here_ref, source_ref, *refs):
    context, out_refs, page_ref, place_ref = refs[: -KV - 2], refs[-KV - 2 : -2], refs[-2], refs[-1]
    pages = source_ref.shape[0]
    slots = pages // (2 * KV)
    here = here_ref[0]
    kind = here % 2
    for page in range(pages):
        place_ref[source_ref[page]] = page
    group = 0
    for ref in context:
        for at in range(ref.shape[0]):
            half, piece = group // KV, group % KV
            device = jnp.bitwise_xor(here, 2 * piece + half)
            for slot in range(slots):
                page = place_ref[device * slots + slot]
                page_ref[page] = ref[at, kind, slot * PAGE : (slot + 1) * PAGE, :]
            group += 1
    for piece, out_ref in enumerate(out_refs):
        first = jnp.bitwise_xor(here // 2, piece) * 2 * slots
        out_ref[...] = page_ref[pl.ds(first, 2 * slots)]


def order_pages(here, source, context):
    pages = source.shape[0]
    return pl.pallas_call(
        pages_kernel,
        out_shape=[shape((pages // KV, PAGE, HD))] * KV,
        in_specs=[SMEM, SMEM] + [VMEM] * len(context),
        out_specs=[VMEM] * KV,
        scratch_shapes=[pltpu.VMEM((pages, PAGE, HD), jnp.bfloat16), pltpu.SMEM((pages,), jnp.int32)],
        name="order_pages",
        compiler_params=params(4),
        cost_estimate=cost(0, 4 * pages * PAGE * HD),
    )(here, source, *context)


def collect_kernel(here_ref, *refs):
    pieces, (keep_ref, send_ref) = refs[:-2], refs[-2:]
    rows = keep_ref.shape[0]
    slots = rows // PAGE
    core = here_ref[0] % 2
    for piece, ref in enumerate(pieces):
        head = jnp.bitwise_xor(here_ref[0] // 2, piece)
        lanes = pl.ds(pl.multiple_of(head * HD, HD), HD)
        keep_ref[:, lanes] = ref[pl.ds(core * slots, slots)].reshape(rows, HD)
        send_ref[:, lanes] = ref[pl.ds((1 - core) * slots, slots)].reshape(rows, HD)


def collect_heads(here, pieces):
    rows = pieces[0].shape[0] * PAGE // 2
    out = shape((rows, KV * HD))
    return pl.pallas_call(
        collect_kernel,
        out_shape=(out, out),
        in_specs=[SMEM] + [VMEM] * KV,
        out_specs=(VMEM, VMEM),
        name="collect_heads",
        compiler_params=params(4),
        cost_estimate=cost(0, 8 * rows * KV * HD),
    )(here, *pieces)


def settle_kernel(here_ref, mine_ref, other_ref, keys_ref, values_ref):
    first = here_ref[0] % 2 == 0
    keys_ref[...] = jnp.where(first, mine_ref[...], other_ref[...])
    values_ref[...] = jnp.where(first, other_ref[...], mine_ref[...])


def settle(here, mine, other):
    return pl.pallas_call(
        settle_kernel,
        out_shape=(shape(mine.shape), shape(mine.shape)),
        in_specs=[SMEM, VMEM, VMEM],
        out_specs=(VMEM, VMEM),
        name="settle",
        compiler_params=params(4),
        cost_estimate=cost(0, 8 * math.prod(mine.shape)),
    )(here, mine, other)


def attention_kernel(pieces, owners, w_ref, *refs):
    s_ref, sems = refs[-2:]
    held = refs[-2 - len(pieces) : -2]
    *refs, out_ref = refs[: -2 - len(pieces)]
    parts = weight_parts(w_ref, pieces, held, owners)
    fetch(parts, sems, lambda: attention_heads(*refs, out_ref, s_ref))


def attention_heads(*refs):
    context, (q_ref, kpos_ref, qpos_ref, out_ref, s_ref) = refs[:-5], refs[-5:]
    count = qpos_ref.shape[1]
    heads = q_ref.shape[0] // count
    rows = context[0].shape[2]
    blocks, at = [], 0
    for ref in context:
        step = max(1, min(ref.shape[0], 512 // rows))
        for first in range(0, ref.shape[0], step):
            blocks.append((ref, slice(first, first + step), slice(at, at + step * rows)))
            at += step * rows
    block = step * rows
    scale = HD**-0.5 * math.log2(math.e)
    qpos = column(qpos_ref[...].astype(jnp.float32))

    def one(head, carry):
        q = q_ref[pl.ds(pl.multiple_of(head * count, count), count), :]
        top = jnp.full((count, HD), masked_score, jnp.float32)
        for ref, chips, lanes in blocks:
            s = lax.dot_general(
                q,
                ref[chips, 0].reshape(block, HD),
                (((1,), (1,)), ((), ())),
                preferred_element_type=jnp.float32,
            )
            s = jnp.where(kpos_ref[:, lanes] <= qpos, s, masked_score)
            s_ref[:, lanes] = s
            for lane in range(0, block, HD):
                top = jnp.maximum(top, s[:, lane : lane + HD])
        top = jnp.max(top, axis=1, keepdims=True)
        total = jnp.zeros((count, HD), jnp.float32)
        summed = jnp.zeros((count, HD), jnp.float32)
        for ref, chips, lanes in blocks:
            w = jnp.exp2((s_ref[:, lanes] - top) * scale)
            for lane in range(0, block, HD):
                total = total + w[:, lane : lane + HD]
            summed = summed + jnp.dot(
                w.astype(jnp.bfloat16),
                ref[chips, 1].reshape(block, HD),
                preferred_element_type=jnp.float32,
            )
        total = jnp.sum(total, axis=1, keepdims=True)
        out_ref[:, pl.ds(pl.multiple_of(head * HD, HD), HD)] = (summed / total).astype(jnp.bfloat16)
        return carry

    lax.fori_loop(0, heads, one, 0, unroll=UNROLL)


def attend(context, q, key_positions, query_positions, out_weight, pieces, owners):
    tokens = key_positions.shape[1]
    count = query_positions.shape[1]
    heads = q.shape[0] // count
    outs = [shape((count, heads * HD))] + weight_shapes(pieces, owners)
    return pl.pallas_call(
        lambda *refs: attention_kernel(pieces, owners, *refs),
        out_shape=outs,
        in_specs=[HBM] + [VMEM] * (len(context) + 3),
        out_specs=[VMEM] * len(outs),
        scratch_shapes=[
            pltpu.VMEM((count, tokens), jnp.float32),
            DMA((len(pieces) * owners,)),
        ],
        name="attend",
        compiler_params=params(6),
        cost_estimate=cost(
            4 * count * heads * tokens * HD, 4 * tokens * HD, count * heads * tokens
        ),
    )(*in_hbm([out_weight]), *context, q, key_positions, query_positions)


def fold_masks(bits):
    masks = [0]
    for bit in reversed(bits):
        masks = masks + [m | bit for m in masks]
    return masks


def columns_of(here_ref, mask, width):
    first = jnp.bitwise_xor(here_ref[0], mask) * width
    return pl.ds(pl.multiple_of(first, HD), width)


def product(x_ref, w_refs, columns):
    total, first = None, 0
    for ref in w_refs:
        last = first + ref.shape[0]
        y = jnp.dot(x_ref[:, first:last], ref[:, columns], preferred_element_type=jnp.float32)
        total = y if total is None else total + y
        first = last
    return total


def project_send_kernel(masks, here_ref, x_ref, *refs):
    *w_refs, out_ref = refs
    for at, mask in enumerate(masks):
        columns = columns_of(here_ref, mask, out_ref.shape[2])
        out_ref[at] = product(x_ref, w_refs, columns).astype(jnp.bfloat16)


def project_keep_kernel(masks, here_ref, x_ref, *refs):
    *w_refs, got_ref, send_ref, keep_ref = refs
    half = len(masks) // 2
    for at in list(range(half, 2 * half)) + list(range(half)):
        columns = columns_of(here_ref, masks[at], got_ref.shape[2])
        y = product(x_ref, w_refs, columns) + got_ref[at].astype(jnp.float32)
        if at >= half:
            send_ref[at - half] = y.astype(jnp.bfloat16)
        else:
            keep_ref[at] = y


def project_cost(x, columns):
    return cost(2 * x.shape[0] * x.shape[1] * columns, 2 * x.shape[1] * columns)


def project_send(here, mixed, weights, masks, width):
    count = mixed.shape[0]
    return pl.pallas_call(
        lambda *refs: project_send_kernel(masks, *refs),
        out_shape=shape((len(masks), count, width)),
        in_specs=[SMEM, VMEM] + [VMEM] * len(weights),
        out_specs=VMEM,
        compiler_params=params(6),
        cost_estimate=project_cost(mixed, len(masks) * width),
    )(here, mixed, *weights)


def project_keep(here, mixed, weights, got, masks):
    count = mixed.shape[0]
    half, width = len(masks) // 2, got.shape[2]
    return pl.pallas_call(
        lambda *refs: project_keep_kernel(masks, *refs),
        out_shape=(shape((half, count, width)), shape((half, count, width), jnp.float32)),
        in_specs=[SMEM, VMEM] + [VMEM] * len(weights) + [VMEM],
        out_specs=(VMEM, VMEM),
        compiler_params=params(6),
        cost_estimate=project_cost(mixed, len(masks) * width),
    )(here, mixed, *weights, got)


def fold_kernel(keep_ref, got_ref, send_ref, left_ref):
    left = left_ref.shape[0]
    for at in range(left):
        send_ref[at] = (keep_ref[left + at] + got_ref[left + at].astype(jnp.float32)).astype(
            jnp.bfloat16
        )
    for at in range(left):
        left_ref[at] = keep_ref[at] + got_ref[at].astype(jnp.float32)


def fold(keep, got):
    owners, count, width = keep.shape
    half = (owners // 2, count, width)
    return pl.pallas_call(
        fold_kernel,
        out_shape=(shape(half), shape(half, jnp.float32)),
        in_specs=[VMEM, VMEM],
        out_specs=(VMEM, VMEM),
        compiler_params=params(4),
        cost_estimate=cost(owners * count * width, 8 * owners * count * width),
    )(keep, got)


def finish_kernel(*refs):
    out_ref, at = refs[-1], 0
    for keep_ref, got_ref in zip(refs[:-1:2], refs[1:-1:2]):
        width = keep_ref.shape[2]
        total = keep_ref[0] + got_ref[0].astype(jnp.float32)
        out_ref[:, at : at + width] = total.astype(jnp.bfloat16)
        at += width


def finish(pairs):
    flat = [x for pair in pairs for x in pair]
    count = flat[0].shape[1]
    width = sum(keep.shape[2] for keep, _ in pairs)
    return pl.pallas_call(
        finish_kernel,
        out_shape=shape((count, width)),
        in_specs=[VMEM] * len(flat),
        out_specs=VMEM,
        name="finish",
        compiler_params=params(4),
        cost_estimate=cost(count * width, 8 * count * width),
    )(*flat)


def swap(x, bits, devices):
    return lax.ppermute(x, "ctx", [(d, d ^ bits) for d in range(devices)])


def after(x, *others):
    return lax.optimization_barrier((x, *others))[0]


def plan(devices, own_width):
    bits = [1 << b for b in range(devices.bit_length() - 1)]
    half = own_width // 2
    return [
        (0, half, bits),
        (half, half, [bits[0], bits[2], bits[1]] + bits[3:]),
    ]


def project_and_scatter(here, devices, x, weights, chunks):
    masks = [fold_masks(order) for _, _, order in chunks]
    half = devices // 2
    state, got = [], []
    for at, (start, width, order) in enumerate(chunks):
        out = project_send(here, x, weights[at], masks[at][half:], width)
        got.append(swap(out, order[0], devices))
        x = after(x, out)
    for at, (start, _, _) in enumerate(chunks):
        send, keep = project_keep(here, x, weights[at], got[at], masks[at][:half])
        state.append((send, keep))
        x = after(x, send)
    stages = len(chunks[0][2])
    for stage in range(1, stages):
        arrived = [swap(send, chunks[at][2][stage], devices) for at, (send, _) in enumerate(state)]
        if stage + 1 < stages:
            state = [fold(keep, got) for (_, keep), got in zip(state, arrived)]
    return finish([(keep, got) for (_, keep), got in zip(state, arrived)])


def body(
    pool_keys,
    pool_values,
    key_scales,
    value_scales,
    page_source,
    page_lengths,
    page_offsets,
    query_positions,
    queries,
    out_weight,
):
    devices = lax.axis_size("ctx")
    here = lax.axis_index("ctx").astype(jnp.int32)[None]
    source, lengths, offsets = page_source[None], page_lengths[None], page_offsets[None]
    positions = query_positions[None]
    pieces = prepare_rows(
        here, pool_keys, pool_values, key_scales, value_scales, source, lengths, offsets
    )
    far = range(KV // 2, KV)
    arrived = [pieces[0]] + [swap(pieces[k], 2 * k, devices) for k in range(1, KV)]
    depth = out_weight.shape[0]
    chunks = plan(devices, out_weight.shape[1] // devices)
    (start, width, _), (later, later_width, _) = chunks
    early_rows = depth * EARLY // 16
    early = [(0, early_rows, later, later_width)]
    late = [(0, depth, start, width)]
    if early_rows < depth:
        late.append((early_rows, depth, later, later_width))
    turned, key_positions, *early_weights = side(
        here, source, lengths, offsets, positions, queries, out_weight, early, devices
    )
    near = assemble(arrived[: KV // 2])
    far = assemble(arrived[KV // 2 :])
    context = [near, far, swap(near, 1, devices), swap(far, 1, devices)]
    leaving = order_pages(here, page_source, context)
    pages = [leaving[0]] + [swap(leaving[k], 2 * k, devices) for k in range(1, KV)]
    mixed, *late_weights = attend(
        context, turned, key_positions, positions, out_weight, late, devices
    )
    output = project_and_scatter(here, devices, mixed, [late_weights[:1], early_weights + late_weights[1:]], chunks)
    mine, partner = collect_heads(here, pages)
    new_keys, new_values = settle(here, mine, swap(partner, 1, devices))
    return (new_keys, new_values, output)


def wide_inverse_freq():
    exponent = jnp.arange(0, HD, 2).astype(jnp.float32) / HD
    base_freq = 1.0 / rope_theta**exponent
    wavelength = 2.0 * math.pi / base_freq
    smooth = (old_context / wavelength - low_factor) / (high_factor - low_factor)
    blended = (1.0 - smooth) * base_freq / scale_factor + smooth * base_freq
    short_wave = wavelength < old_context / high_factor
    longer = wavelength > old_context / low_factor
    return jnp.where(short_wave, base_freq, jnp.where(longer, base_freq / scale_factor, blended))


def rotate(values, positions):
    angle = positions.astype(jnp.float32)[:, None] * wide_inverse_freq()[None, :]
    cosine = jnp.cos(angle)[:, None, :]
    sine_part = jnp.sin(angle)[:, None, :]
    half_size = values.shape[-1] // 2
    first_half = values[..., :half_size]
    second = values[..., half_size:]
    return jnp.concatenate(
        [first_half * cosine - second * sine_part, second * cosine + first_half * sine_part],
        axis=-1,
    )


def wide_body(
    pool_keys,
    pool_values,
    key_scales,
    value_scales,
    page_source,
    page_lengths,
    page_offsets,
    query_positions,
    queries,
    out_weight,
):
    devices = lax.axis_size("ctx")
    here_index = lax.axis_index("ctx")
    slot_count = key_scales.shape[0]
    page_count = page_source.shape[0]
    query_count = queries.shape[0]
    local_heads = queries.shape[1] // HD
    per_group = H // KV
    in_page = jnp.arange(PAGE, dtype=jnp.int32)
    inverse = (
        jnp.zeros((page_count,), jnp.int32)
        .at[page_source]
        .set(jnp.arange(page_count, dtype=jnp.int32))
    )
    held_pages = lax.dynamic_slice_in_dim(inverse, here_index * slot_count, slot_count)
    held_live = in_page[None, :] < page_lengths[held_pages][:, None]
    live_float = held_live.reshape(-1).astype(jnp.float32)[:, None, None]
    scaled_keys = (
        pool_keys.reshape(slot_count, PAGE, KV, HD).astype(jnp.float32)
        * key_scales[:, None, :, None]
    )
    scaled_values = (
        pool_values.reshape(slot_count, PAGE, KV, HD).astype(jnp.float32)
        * value_scales[:, None, :, None]
    )
    turned = rotate(
        scaled_keys.reshape(slot_count * PAGE, KV, HD), jnp.repeat(page_offsets[held_pages], PAGE)
    )
    slot_keys = (turned * live_float).astype(jnp.bfloat16).reshape(slot_count, PAGE * KV * HD)
    slot_values = (
        (scaled_values.reshape(slot_count * PAGE, KV, HD) * live_float)
        .astype(jnp.bfloat16)
        .reshape(slot_count, PAGE * KV * HD)
    )
    owner_device = held_pages // slot_count
    routing = (owner_device[None, :] == jnp.arange(devices, dtype=jnp.int32)[:, None]).astype(
        jnp.bfloat16
    )
    outgoing_keys = jnp.dot(routing, slot_keys, preferred_element_type=jnp.float32).astype(
        jnp.bfloat16
    )
    outgoing_values = jnp.dot(routing, slot_values, preferred_element_type=jnp.float32).astype(
        jnp.bfloat16
    )
    arrived_keys, arrived_values = (
        lax.all_to_all(outgoing_keys, "ctx", split_axis=0, concat_axis=0, tiled=True),
        lax.all_to_all(outgoing_values, "ctx", split_axis=0, concat_axis=0, tiled=True),
    )
    assembled_pages = here_index * slot_count + jnp.arange(slot_count, dtype=jnp.int32)
    sender = page_source[assembled_pages] // slot_count
    new_keys = arrived_keys[sender].reshape(slot_count * PAGE, KV * HD)
    new_values = arrived_values[sender].reshape(slot_count * PAGE, KV * HD)
    local_keys = slot_keys.reshape(slot_count * PAGE, KV * HD)
    local_values = slot_values.reshape(slot_count * PAGE, KV * HD)
    local_tokens = local_keys.shape[0]
    turned_q = rotate(
        queries.astype(jnp.float32).reshape(query_count, local_heads, HD), query_positions
    )
    own_queries = turned_q.astype(jnp.bfloat16).transpose(1, 0, 2)
    target = jnp.arange(devices, dtype=jnp.int32) * local_heads // per_group
    keys_by_head = local_keys.reshape(local_tokens, KV, HD).transpose(1, 0, 2)
    values_by_head = local_values.reshape(local_tokens, KV, HD).transpose(1, 0, 2)
    head_keys, head_values = (
        lax.all_to_all(keys_by_head[target], "ctx", split_axis=0, concat_axis=0, tiled=True),
        lax.all_to_all(values_by_head[target], "ctx", split_axis=0, concat_axis=0, tiled=True),
    )
    key_positions = (page_offsets[inverse][:, None] + in_page[None, :]).reshape(-1)
    key_live = (in_page[None, :] < page_lengths[inverse][:, None]).reshape(-1)
    key_positions, key_live = (key_positions, key_live)
    allowed = (key_positions[None, :] <= query_positions[:, None]) & key_live[None, :]
    span_devices = max(1, min(devices, 4096 // local_tokens))
    while span_devices > 1 and devices % span_devices:
        span_devices -= 1
    block_count = devices // span_devices
    key_blocks = head_keys.reshape(block_count, span_devices * local_tokens, HD)
    value_blocks = head_values.reshape(block_count, span_devices * local_tokens, HD)
    allowed_blocks = allowed.reshape(
        query_count, block_count, span_devices * local_tokens
    ).transpose(1, 0, 2)

    def block_scores(key_block, allow_block):
        scores = jnp.einsum(
            "hqd,kd->hqk", own_queries, key_block, preferred_element_type=jnp.float32
        ) * HD ** (-0.5)
        return jnp.where(allow_block[None], scores, masked_score)

    block_max = lax.map(
        lambda operands: jnp.max(block_scores(operands[0], operands[1]), axis=-1),
        (key_blocks, allowed_blocks),
    )
    row_max = jnp.max(block_max, axis=0)

    def weigh_block(operands):
        key_block, value_block, allow_block = operands
        weights = jnp.exp(block_scores(key_block, allow_block) - row_max[..., None])
        denominator = jnp.sum(weights, axis=-1)
        summed = jnp.einsum(
            "hqk,kd->hqd",
            weights.astype(jnp.bfloat16),
            value_block,
            preferred_element_type=jnp.float32,
        )
        return (summed, denominator)

    summed, denominator = lax.map(weigh_block, (key_blocks, value_blocks, allowed_blocks))
    summed = jnp.sum(summed, axis=0)
    denominator = jnp.sum(denominator, axis=0)
    attended = (summed / denominator[..., None]).astype(jnp.bfloat16)
    mixed = attended.transpose(1, 0, 2).reshape(query_count, local_heads * HD)
    reduced = lax.psum_scatter(
        lax.dot_general(
            out_weight, mixed, (((0,), (1,)), ((), ())), preferred_element_type=jnp.float32
        ),
        "ctx",
        scatter_dimension=0,
        tiled=True,
    )
    output = reduced.T.astype(jnp.bfloat16)
    return (new_keys, new_values, output)


def solution(mesh):
    in_specs = (
        P(("groups", "ctx"), None),
        P(("groups", "ctx"), None),
        P(("groups", "ctx"), None),
        P(("groups", "ctx"), None),
        P("groups"),
        P("groups"),
        P("groups"),
        P("groups"),
        P("groups", "ctx"),
        P("ctx", None),
    )
    out_specs = (P(("groups", "ctx"), None), P(("groups", "ctx"), None), P("groups", "ctx"))
    fits = mesh.shape["ctx"] == 2 * KV
    chosen = body if fits else wide_body
    return jax.shard_map(
        chosen, mesh=mesh, in_specs=in_specs, out_specs=out_specs, check_vma=False
    )
```

```python
import math

import jax
import jax.numpy as jnp
import numpy as np
from jax import lax
from jax.experimental import pallas as pl
from jax.experimental.pallas import tpu as pltpu
from jax.sharding import PartitionSpec as P


H = 128
KV = 8
HD = 128
PAGE = 16
MIB = 1 << 20
BLOCK = 512
HEADS_AT_ONCE = 2
SHARE = 4


rope_theta = 500000.0
scale_factor = 8.0
low_factor = 1.0
high_factor = 4.0
old_context = 8192.0
masked_score = -1e30
far_position = 1e9
VMEM = pl.BlockSpec(memory_space=pltpu.VMEM)
SMEM = pl.BlockSpec(memory_space=pltpu.SMEM)
HBM = pl.BlockSpec(memory_space=pltpu.HBM)
DMA = pltpu.SemaphoreType.DMA


def inverse_freq():
    exponent = np.arange(0, HD, 2).astype(np.float64) / HD
    base_freq = 1.0 / rope_theta**exponent
    wavelength = 2.0 * math.pi / base_freq
    smooth = (old_context / wavelength - low_factor) / (high_factor - low_factor)
    blended = (1.0 - smooth) * base_freq / scale_factor + smooth * base_freq
    short_wave = wavelength < old_context / high_factor
    longer = wavelength > old_context / low_factor
    return np.where(
        short_wave, base_freq, np.where(longer, base_freq / scale_factor, blended)
    ).astype(np.float32)


def lane_tables():
    freq = inverse_freq()
    sign = np.repeat([-1.0, 1.0], HD // 2)
    return jnp.asarray(np.stack([np.concatenate([freq, freq]), sign]).astype(np.float32))


def params(mib):
    return pltpu.CompilerParams(vmem_limit_bytes=mib * MIB)


def cost(flops, moved, exps=0):
    return pl.CostEstimate(flops=flops, bytes_accessed=moved, transcendentals=exps)


def shape(dims, dtype=jnp.bfloat16):
    return jax.ShapeDtypeStruct(dims, dtype)


def cos_sin(position, table_ref):
    angle = position * table_ref[0:1, :]
    return jnp.cos(angle), jnp.sin(angle) * table_ref[1:2, :]


def turn(x, cosine, sine):
    return x * cosine + pltpu.roll(x, HD // 2, 1) * sine


def column(row):
    n = row.shape[1]
    same = lax.broadcasted_iota(jnp.int32, (n, n), 0) == lax.broadcasted_iota(jnp.int32, (n, n), 1)
    return jnp.sum(jnp.where(same, row, 0.0), axis=1, keepdims=True)


def fetch(pairs, sems, meanwhile=None):
    copies = [pltpu.make_async_copy(a, b, sems.at[at]) for at, (a, b) in enumerate(pairs)]
    for copy in copies:
        copy.start()
    if meanwhile is not None:
        meanwhile()
    for copy in copies:
        copy.wait()


def in_hbm(xs):
    return [pltpu.with_memory_space_constraint(x, pltpu.HBM) for x in xs]


def vmem_like(x):
    return pltpu.VMEM(x.shape, x.dtype)


def rows_kernel(pieces, owners, here_ref, w_ref, *refs):
    inputs, outs, scratch = refs[:8], refs[8:-10], refs[-10:-2]
    sems, weight_sems = refs[-2:]

    def compute():
        fetch_and_turn(here_ref, inputs, scratch, sems, outs[:KV])

    fetch(weight_parts(w_ref, pieces, outs[KV:], owners), weight_sems, compute)


def fetch_and_turn(here_ref, inputs, scratch, sems, out_refs):
    fetch(list(zip(inputs, scratch)), sems)
    ks_ref, vs_ref, table_ref, source_ref, lengths_ref, offsets_ref, pk_ref, pv_ref = scratch
    rows = pk_ref.shape[0]
    slots = rows // PAGE
    pages = source_ref.shape[1]
    row = lax.broadcasted_iota(jnp.int32, (rows, pages), 0)
    match = source_ref[...] == here_ref[0] * slots + row // PAGE

    def pick(ref):
        return jnp.sum(jnp.where(match, ref[...].astype(jnp.float32), 0.0), axis=1, keepdims=True)

    position, length = pick(offsets_ref), pick(lengths_ref)
    cosine, sine = cos_sin(position, table_ref)
    token = (lax.broadcasted_iota(jnp.int32, (rows, 1), 0) % PAGE).astype(jnp.float32)
    live = jnp.broadcast_to((token < length).astype(jnp.float32), (rows, HD))
    for piece, out_ref in enumerate(out_refs):
        head = jnp.bitwise_xor(here_ref[0] // 2, piece)
        lanes = pl.ds(pl.multiple_of(head * HD, HD), HD)
        for slot in range(slots):
            part = slice(slot * PAGE, (slot + 1) * PAGE)
            k = pk_ref[part, lanes].astype(jnp.float32) * ks_ref[slot, head]
            k = turn(k, cosine[part], sine[part]) * live[part]
            out_ref[0, part, :] = k.astype(jnp.bfloat16)
            v = pv_ref[part, lanes].astype(jnp.float32) * vs_ref[slot, head]
            out_ref[1, part, :] = (v * live[part]).astype(jnp.bfloat16)


def prepare_rows(here, out_weight, pieces, owners, *tables):
    pool_keys, pool_values, key_scales, value_scales, source, lengths, offsets = tables
    rows = pool_keys.shape[0]
    table = lane_tables()
    small = [pltpu.SMEM(key_scales.shape, jnp.float32)] * 2
    inputs = (key_scales, value_scales, table, source, lengths, offsets, pool_keys, pool_values)
    outs = [shape((2, rows, HD))] * KV + weight_shapes(pieces, owners)
    sems = [DMA((8,)), DMA((max(1, len(pieces)) * owners,))]
    return pl.pallas_call(
        lambda *refs: rows_kernel(pieces, owners, *refs),
        out_shape=outs,
        in_specs=[SMEM] + [HBM] * 9,
        out_specs=[VMEM] * len(outs),
        scratch_shapes=small + [vmem_like(x) for x in inputs[2:]] + sems,
        name="prepare_rows",
        compiler_params=params(6),
        cost_estimate=cost(20 * rows * KV * HD, 8 * rows * KV * HD),
    )(here, *in_hbm((out_weight, *inputs)))


def weight_parts(w_ref, pieces, refs, owners):
    own_width = w_ref.shape[1] // owners
    parts = []
    for (first, last, start, width), ref in zip(pieces, refs):
        for owner in range(owners):
            columns = pl.ds(owner * own_width + start, width)
            parts.append(
                (w_ref.at[first:last, columns], ref.at[:, pl.ds(owner * width, width)])
            )
    return parts


def weight_shapes(pieces, owners):
    return [shape((last - first, owners * width)) for first, last, _, width in pieces]


def side_kernel(pieces, owners, here_ref, w_ref, *refs):
    inputs, outs, refs = refs[:6], refs[6:8], refs[8:]
    held, scratch, sems, weight_sems = refs[: len(pieces)], refs[len(pieces) : -2], refs[-2], refs[-1]

    def compute():
        fetch(list(zip(inputs, scratch)), sems)
        side_rows(here_ref, *scratch, *outs)

    fetch(weight_parts(w_ref, pieces, held, owners), weight_sems, compute)


def side_rows(here_ref, *refs):
    (out_ref, kpos_ref), scratch = refs[-2:], refs[:-2]
    table_ref, source_ref, lengths_ref, offsets_ref, position_ref, q_ref = scratch
    count = q_ref.shape[0]
    cosine, sine = cos_sin(column(position_ref[...].astype(jnp.float32)), table_ref)
    for head in range(q_ref.shape[1] // HD):
        q = q_ref[:, head * HD : (head + 1) * HD].astype(jnp.float32)
        out_ref[head * count : (head + 1) * count, :] = turn(q, cosine, sine).astype(jnp.bfloat16)
    source = column(source_ref[...].astype(jnp.float32))
    length = column(lengths_ref[...].astype(jnp.float32))
    offset = column(offsets_ref[...].astype(jnp.float32))
    tokens = kpos_ref.shape[1]
    rows = tokens // (2 * KV)
    slots = rows // PAGE
    at = lax.broadcasted_iota(jnp.int32, (1, rows), 1)
    token = (at % PAGE).astype(jnp.float32)
    where = jnp.where(token < length, offset + token, far_position)
    for group in range(2 * KV):
        half, piece = group // KV, group % KV
        device = jnp.bitwise_xor(here_ref[0], 2 * piece + half)
        page = (device * slots + at // PAGE).astype(jnp.float32)
        kpos_ref[:, group * rows : (group + 1) * rows] = jnp.sum(
            jnp.where(source == page, where, 0.0), axis=0, keepdims=True
        )


def side(here, source, lengths, offsets, positions, queries, out_weight, pieces, owners):
    count, width = queries.shape
    tokens = source.shape[1] * PAGE
    inputs = (lane_tables(), source, lengths, offsets, positions, queries)
    outs = [shape((count * (width // HD), HD)), shape((1, tokens), jnp.float32)]
    outs += weight_shapes(pieces, owners)
    return pl.pallas_call(
        lambda *refs: side_kernel(pieces, owners, *refs),
        out_shape=outs,
        in_specs=[SMEM] + [HBM] * 7,
        out_specs=[VMEM] * len(outs),
        scratch_shapes=[vmem_like(x) for x in inputs] + [DMA((6,)), DMA((len(pieces) * owners,))],
        name="side",
        compiler_params=params(6),
        cost_estimate=cost(8 * count * width, 64 * MIB),
    )(here, *in_hbm((out_weight, *inputs)))


def assemble_kernel(*refs):
    for at, ref in enumerate(refs[:-1]):
        refs[-1][at] = ref[...]


def assemble(pieces):
    dims = (len(pieces), *pieces[0].shape)
    return pl.pallas_call(
        assemble_kernel,
        out_shape=shape(dims),
        in_specs=[VMEM] * len(pieces),
        out_specs=VMEM,
        compiler_params=params(2),
        cost_estimate=cost(0, 4 * math.prod(dims)),
    )(*pieces)


def pages_kernel(here_ref, source_ref, *refs):
    *context, near_ref, far_ref, page_ref, place_ref = refs
    pages = source_ref.shape[0]
    slots = pages // (2 * KV)
    here = here_ref[0]
    kind = here % 2
    for page in range(pages):
        place_ref[source_ref[page]] = page
    group = 0
    for ref in context:
        for at in range(ref.shape[0]):
            half, piece = group // KV, group % KV
            device = jnp.bitwise_xor(here, 2 * piece + half)
            for slot in range(slots):
                page = place_ref[device * slots + slot]
                page_ref[page] = ref[at, kind, slot * PAGE : (slot + 1) * PAGE, :]
            group += 1
    for piece in range(KV):
        first = jnp.bitwise_xor(here // 2, piece) * 2 * slots
        out_ref = near_ref if piece < KV // 2 else far_ref
        out_ref[piece % (KV // 2)] = page_ref[pl.ds(first, 2 * slots)]


def order_pages(here, source, context):
    pages = source.shape[0]
    return pl.pallas_call(
        pages_kernel,
        out_shape=[shape((KV // 2, pages // KV, PAGE, HD))] * 2,
        in_specs=[SMEM, SMEM] + [VMEM] * len(context),
        out_specs=[VMEM] * 2,
        scratch_shapes=[pltpu.VMEM((pages, PAGE, HD), jnp.bfloat16), pltpu.SMEM((pages,), jnp.int32)],
        name="order_pages",
        compiler_params=params(4),
        cost_estimate=cost(0, 4 * pages * PAGE * HD),
    )(here, source, *context)


def forward_kernel(first, *refs):
    *held, out_ref = refs
    at = 0
    for ref in held:
        for row in range(ref.shape[0]):
            out_ref[at] = ref[row, first : first + out_ref.shape[1]]
            at += 1


def forward(held, first):
    count = sum(x.shape[0] for x in held)
    dims = (count, first, *held[0].shape[2:])
    return pl.pallas_call(
        lambda *refs: forward_kernel(first, *refs),
        out_shape=shape(dims),
        in_specs=[VMEM] * len(held),
        out_specs=VMEM,
        compiler_params=params(4),
        cost_estimate=cost(0, 4 * math.prod(dims)),
    )(*held)


def send_pages(near, far, devices):
    held, heads = [near[None]], [0]
    send = far[None]
    bit = KV // 2
    while True:
        held.append(swap(send, 2 * bit, devices))
        heads += [head | bit for head in heads]
        bit //= 2
        if not bit:
            break
        send = forward(held, bit)
    return held, heads


def collect_kernel(heads, here_ref, *refs):
    *held, keep_ref, send_ref = refs
    rows = keep_ref.shape[0]
    slots = rows // PAGE
    core = here_ref[0] % 2
    pieces = [(ref, row) for ref in held for row in range(ref.shape[0])]
    for (ref, row), apart in zip(pieces, heads):
        head = jnp.bitwise_xor(here_ref[0] // 2, apart)
        lanes = pl.ds(pl.multiple_of(head * HD, HD), HD)
        keep_ref[:, lanes] = ref[row, 0, pl.ds(core * slots, slots)].reshape(rows, HD)
        send_ref[:, lanes] = ref[row, 0, pl.ds((1 - core) * slots, slots)].reshape(rows, HD)


def collect_heads(here, held, heads):
    rows = held[0].shape[2] * PAGE // 2
    out = shape((rows, KV * HD))
    return pl.pallas_call(
        lambda *refs: collect_kernel(heads, *refs),
        out_shape=(out, out),
        in_specs=[SMEM] + [VMEM] * len(held),
        out_specs=(VMEM, VMEM),
        name="collect_heads",
        compiler_params=params(4),
        cost_estimate=cost(0, 8 * rows * KV * HD),
    )(here, *held)


def settle_kernel(here_ref, mine_ref, other_ref, keys_ref, values_ref):
    first = here_ref[0] % 2 == 0
    keys_ref[...] = jnp.where(first, mine_ref[...], other_ref[...])
    values_ref[...] = jnp.where(first, other_ref[...], mine_ref[...])


def settle(here, mine, other):
    return pl.pallas_call(
        settle_kernel,
        out_shape=(shape(mine.shape), shape(mine.shape)),
        in_specs=[SMEM, VMEM, VMEM],
        out_specs=(VMEM, VMEM),
        name="settle",
        compiler_params=params(4),
        cost_estimate=cost(0, 8 * math.prod(mine.shape)),
    )(here, mine, other)


def attention_kernel(pieces, owners, w_ref, *refs):
    s_ref, sems = refs[-2:]
    held = refs[-2 - len(pieces) : -2]
    *refs, out_ref = refs[: -2 - len(pieces)]
    parts = weight_parts(w_ref, pieces, held, owners)
    fetch(parts, sems, lambda: attention_heads(*refs, out_ref, s_ref))


def attention_heads(*refs):
    context, (q_ref, kpos_ref, qpos_ref, out_ref, s_ref) = refs[:-5], refs[-5:]
    count = qpos_ref.shape[1]
    heads = q_ref.shape[0] // count
    group = s_ref.shape[0] // count
    rows = context[0].shape[2]
    blocks, at = [], 0
    for ref in context:
        step = max(1, min(ref.shape[0], BLOCK // rows))
        for first in range(0, ref.shape[0], step):
            blocks.append((ref, slice(first, first + step), slice(at, at + step * rows)))
            at += step * rows
    block = step * rows
    scale = HD**-0.5 * math.log2(math.e)
    qpos = column(qpos_ref[...].astype(jnp.float32))
    qpos = jnp.concatenate([qpos] * group, axis=0)
    size = group * count

    def one(index, carry):
        q = q_ref[pl.ds(pl.multiple_of(index * size, size), size), :]
        top = jnp.full((size, HD), masked_score, jnp.float32)
        for ref, chips, lanes in blocks:
            s = lax.dot_general(
                q,
                ref[chips, 0].reshape(block, HD),
                (((1,), (1,)), ((), ())),
                preferred_element_type=jnp.float32,
            )
            s = jnp.where(kpos_ref[:, lanes] <= qpos, s, masked_score)
            s_ref[:, lanes] = s
            for lane in range(0, block, HD):
                top = jnp.maximum(top, s[:, lane : lane + HD])
        top = jnp.max(top, axis=1, keepdims=True)
        total = jnp.zeros((size, HD), jnp.float32)
        summed = jnp.zeros((size, HD), jnp.float32)
        for ref, chips, lanes in blocks:
            w = jnp.exp2((s_ref[:, lanes] - top) * scale)
            for lane in range(0, block, HD):
                total = total + w[:, lane : lane + HD]
            summed = summed + jnp.dot(
                w.astype(jnp.bfloat16),
                ref[chips, 1].reshape(block, HD),
                preferred_element_type=jnp.float32,
            )
        out = (summed / jnp.sum(total, axis=1, keepdims=True)).astype(jnp.bfloat16)
        for at in range(group):
            lanes = pl.ds(pl.multiple_of((index * group + at) * HD, HD), HD)
            out_ref[:, lanes] = out[at * count : (at + 1) * count]
        return carry

    lax.fori_loop(0, heads // group, one, 0, unroll=2)


def attend(context, q, key_positions, query_positions, out_weight, pieces, owners):
    tokens = key_positions.shape[1]
    count = query_positions.shape[1]
    heads = q.shape[0] // count
    outs = [shape((count, heads * HD))] + weight_shapes(pieces, owners)
    return pl.pallas_call(
        lambda *refs: attention_kernel(pieces, owners, *refs),
        out_shape=outs,
        in_specs=[HBM] + [VMEM] * (len(context) + 3),
        out_specs=[VMEM] * len(outs),
        scratch_shapes=[
            pltpu.VMEM((math.gcd(heads, HEADS_AT_ONCE) * count, tokens), jnp.float32),
            DMA((len(pieces) * owners,)),
        ],
        name="attend",
        compiler_params=params(8),
        cost_estimate=cost(
            4 * count * heads * tokens * HD, 4 * tokens * HD, count * heads * tokens
        ),
    )(*in_hbm([out_weight]), *context, q, key_positions, query_positions)


def fold_masks(bits):
    masks = [0]
    for bit in reversed(bits):
        masks = masks + [m | bit for m in masks]
    return masks


def columns_of(here_ref, mask, width):
    first = jnp.bitwise_xor(here_ref[0], mask) * width
    return pl.ds(pl.multiple_of(first, HD), width)


def product(x_ref, w_refs, columns):
    total, first = None, 0
    for ref in w_refs:
        last = first + ref.shape[0]
        y = jnp.dot(x_ref[:, first:last], ref[:, columns], preferred_element_type=jnp.float32)
        total = y if total is None else total + y
        first = last
    return total


def project_send_kernel(masks, pieces, owners, here_ref, w_ref, x_ref, *refs):
    held, sems = refs[len(refs) - 1 - len(pieces) : -1], refs[-1]
    *w_refs, out_ref = refs[: len(refs) - 1 - len(pieces)]

    def compute():
        for at, mask in enumerate(masks):
            columns = columns_of(here_ref, mask, out_ref.shape[2])
            out_ref[at] = product(x_ref, w_refs, columns).astype(jnp.bfloat16)

    fetch(weight_parts(w_ref, pieces, held, owners), sems, compute)


def project_add_kernel(masks, first, here_ref, x_ref, *refs):
    *w_refs, got_ref, out_ref = refs
    for at, mask in enumerate(masks):
        columns = columns_of(here_ref, mask, got_ref.shape[2])
        y = product(x_ref, w_refs, columns) + got_ref[first + at].astype(jnp.float32)
        out_ref[at] = y.astype(out_ref.dtype)


def project_cost(x, columns):
    return cost(2 * x.shape[0] * x.shape[1] * columns, 2 * x.shape[1] * columns)


def project_send(here, mixed, weights, masks, width, out_weight, pieces, owners):
    count = mixed.shape[0]
    outs = [shape((len(masks), count, width))] + weight_shapes(pieces, owners)
    return pl.pallas_call(
        lambda *refs: project_send_kernel(masks, pieces, owners, *refs),
        out_shape=outs,
        in_specs=[SMEM, HBM, VMEM] + [VMEM] * len(weights),
        out_specs=[VMEM] * len(outs),
        scratch_shapes=[DMA((max(1, len(pieces)) * owners,))],
        compiler_params=params(6),
        cost_estimate=project_cost(mixed, len(masks) * width),
    )(here, *in_hbm([out_weight]), mixed, *weights)


def project_add(here, mixed, weights, got, masks, first, dtype):
    count = mixed.shape[0]
    width = got.shape[2]
    return pl.pallas_call(
        lambda *refs: project_add_kernel(masks, first, *refs),
        out_shape=shape((len(masks), count, width), dtype),
        in_specs=[SMEM, VMEM] + [VMEM] * len(weights) + [VMEM],
        out_specs=VMEM,
        compiler_params=params(6),
        cost_estimate=project_cost(mixed, len(masks) * width),
    )(here, mixed, *weights, got)


def fold_kernel(keep_ref, got_ref, send_ref, left_ref):
    left = left_ref.shape[0]
    for at in range(left):
        send_ref[at] = (keep_ref[left + at] + got_ref[left + at].astype(jnp.float32)).astype(
            jnp.bfloat16
        )
    for at in range(left):
        left_ref[at] = keep_ref[at] + got_ref[at].astype(jnp.float32)


def fold(keep, got):
    owners, count, width = keep.shape
    half = (owners // 2, count, width)
    return pl.pallas_call(
        fold_kernel,
        out_shape=(shape(half), shape(half, jnp.float32)),
        in_specs=[VMEM, VMEM],
        out_specs=(VMEM, VMEM),
        compiler_params=params(4),
        cost_estimate=cost(owners * count * width, 8 * owners * count * width),
    )(keep, got)


def finish_kernel(*refs):
    out_ref, at = refs[-1], 0
    for keep_ref, got_ref in zip(refs[:-1:2], refs[1:-1:2]):
        width = keep_ref.shape[2]
        total = keep_ref[0] + got_ref[0].astype(jnp.float32)
        out_ref[:, at : at + width] = total.astype(jnp.bfloat16)
        at += width


def finish(pairs):
    flat = [x for pair in pairs for x in pair]
    count = flat[0].shape[1]
    width = sum(keep.shape[2] for keep, _ in pairs)
    return pl.pallas_call(
        finish_kernel,
        out_shape=shape((count, width)),
        in_specs=[VMEM] * len(flat),
        out_specs=VMEM,
        name="finish",
        compiler_params=params(4),
        cost_estimate=cost(count * width, 8 * count * width),
    )(*flat)


def swap(x, bits, devices):
    return lax.ppermute(x, "ctx", [(d, d ^ bits) for d in range(devices)])


def after(x, *others):
    return lax.optimization_barrier((x, *others))[0]


def plan(devices, own_width):
    bits = [1 << b for b in range(devices.bit_length() - 1)]
    first = own_width * SHARE // 8
    return [
        (0, first, bits),
        (first, own_width - first, [bits[0], bits[2], bits[1]] + bits[3:]),
    ]


def project_and_scatter(here, devices, x, out_weight, weights, chunks, last):
    masks = [fold_masks(order) for _, _, order in chunks]
    half, quarter = devices // 2, devices // 4
    got, sends, keeps = [], [], []
    weights = [list(w) for w in weights]
    for at, (_, width, order) in enumerate(chunks):
        out, *more = project_send(
            here, x, weights[at], masks[at][half:], width, out_weight, last[at], devices
        )
        if more:
            weights[at + 1] += more
        got.append(swap(out, order[0], devices))
        x = after(x, out)
    for dtype, into, first in ((jnp.bfloat16, sends, quarter), (jnp.float32, keeps, 0)):
        for at, w in enumerate(weights):
            part = masks[at][first : first + quarter]
            y = project_add(here, x, w, got[at], part, first, dtype)
            into.append(y)
            x = after(x, y)
    state = list(zip(sends, keeps))
    stages = len(chunks[0][2])
    for stage in range(1, stages):
        arrived = [swap(send, chunks[at][2][stage], devices) for at, (send, _) in enumerate(state)]
        if stage + 1 < stages:
            state = [fold(keep, got) for (_, keep), got in zip(state, arrived)]
    return finish([(keep, got) for (_, keep), got in zip(state, arrived)])


def body(
    pool_keys,
    pool_values,
    key_scales,
    value_scales,
    page_source,
    page_lengths,
    page_offsets,
    query_positions,
    queries,
    out_weight,
):
    devices = lax.axis_size("ctx")
    here = lax.axis_index("ctx").astype(jnp.int32)[None]
    source, lengths, offsets = page_source[None], page_lengths[None], page_offsets[None]
    positions = query_positions[None]
    depth = out_weight.shape[0]
    chunks = plan(devices, out_weight.shape[1] // devices)
    first_part, send_part = [], []
    attention_part, side_part = [
        [(0, depth, start, width)] for start, width, _ in chunks
    ]
    prepared = prepare_rows(
        here,
        out_weight,
        first_part,
        devices,
        pool_keys,
        pool_values,
        key_scales,
        value_scales,
        source,
        lengths,
        offsets,
    )
    pieces, first_weights = prepared[:KV], prepared[KV:]
    far = range(KV // 2, KV)
    arrived = [pieces[0]] + [swap(pieces[k], 2 * k, devices) for k in range(1, KV)]
    turned, key_positions, *side_weights = side(
        here, source, lengths, offsets, positions, queries, out_weight, side_part, devices
    )
    near = assemble(arrived[: KV // 2])
    far = assemble(arrived[KV // 2 :])
    context = [near, far, swap(near, 1, devices), swap(far, 1, devices)]
    near_pages, far_pages = order_pages(here, page_source, context)
    held, heads = send_pages(near_pages, far_pages, devices)
    mixed, *late_weights = attend(
        context, turned, key_positions, positions, out_weight, attention_part, devices
    )
    output = project_and_scatter(
        here,
        devices,
        mixed,
        out_weight,
        [[*first_weights, *late_weights], side_weights],
        chunks,
        [send_part, []],
    )
    mine, partner = collect_heads(here, held, heads)
    new_keys, new_values = settle(here, mine, swap(partner, 1, devices))
    return (new_keys, new_values, output)


def wide_inverse_freq():
    exponent = jnp.arange(0, HD, 2).astype(jnp.float32) / HD
    base_freq = 1.0 / rope_theta**exponent
    wavelength = 2.0 * math.pi / base_freq
    smooth = (old_context / wavelength - low_factor) / (high_factor - low_factor)
    blended = (1.0 - smooth) * base_freq / scale_factor + smooth * base_freq
    short_wave = wavelength < old_context / high_factor
    longer = wavelength > old_context / low_factor
    return jnp.where(short_wave, base_freq, jnp.where(longer, base_freq / scale_factor, blended))


def rotate(values, positions):
    angle = positions.astype(jnp.float32)[:, None] * wide_inverse_freq()[None, :]
    cosine = jnp.cos(angle)[:, None, :]
    sine_part = jnp.sin(angle)[:, None, :]
    half_size = values.shape[-1] // 2
    first_half = values[..., :half_size]
    second = values[..., half_size:]
    return jnp.concatenate(
        [first_half * cosine - second * sine_part, second * cosine + first_half * sine_part],
        axis=-1,
    )


def wide_body(
    pool_keys,
    pool_values,
    key_scales,
    value_scales,
    page_source,
    page_lengths,
    page_offsets,
    query_positions,
    queries,
    out_weight,
):
    devices = lax.axis_size("ctx")
    here_index = lax.axis_index("ctx")
    slot_count = key_scales.shape[0]
    page_count = page_source.shape[0]
    query_count = queries.shape[0]
    local_heads = queries.shape[1] // HD
    per_group = H // KV
    in_page = jnp.arange(PAGE, dtype=jnp.int32)
    inverse = (
        jnp.zeros((page_count,), jnp.int32)
        .at[page_source]
        .set(jnp.arange(page_count, dtype=jnp.int32))
    )
    held_pages = lax.dynamic_slice_in_dim(inverse, here_index * slot_count, slot_count)
    held_live = in_page[None, :] < page_lengths[held_pages][:, None]
    live_float = held_live.reshape(-1).astype(jnp.float32)[:, None, None]
    scaled_keys = (
        pool_keys.reshape(slot_count, PAGE, KV, HD).astype(jnp.float32)
        * key_scales[:, None, :, None]
    )
    scaled_values = (
        pool_values.reshape(slot_count, PAGE, KV, HD).astype(jnp.float32)
        * value_scales[:, None, :, None]
    )
    turned = rotate(
        scaled_keys.reshape(slot_count * PAGE, KV, HD), jnp.repeat(page_offsets[held_pages], PAGE)
    )
    slot_keys = (turned * live_float).astype(jnp.bfloat16).reshape(slot_count, PAGE * KV * HD)
    slot_values = (
        (scaled_values.reshape(slot_count * PAGE, KV, HD) * live_float)
        .astype(jnp.bfloat16)
        .reshape(slot_count, PAGE * KV * HD)
    )
    owner_device = held_pages // slot_count
    routing = (owner_device[None, :] == jnp.arange(devices, dtype=jnp.int32)[:, None]).astype(
        jnp.bfloat16
    )
    outgoing_keys = jnp.dot(routing, slot_keys, preferred_element_type=jnp.float32).astype(
        jnp.bfloat16
    )
    outgoing_values = jnp.dot(routing, slot_values, preferred_element_type=jnp.float32).astype(
        jnp.bfloat16
    )
    arrived_keys, arrived_values = (
        lax.all_to_all(outgoing_keys, "ctx", split_axis=0, concat_axis=0, tiled=True),
        lax.all_to_all(outgoing_values, "ctx", split_axis=0, concat_axis=0, tiled=True),
    )
    assembled_pages = here_index * slot_count + jnp.arange(slot_count, dtype=jnp.int32)
    sender = page_source[assembled_pages] // slot_count
    new_keys = arrived_keys[sender].reshape(slot_count * PAGE, KV * HD)
    new_values = arrived_values[sender].reshape(slot_count * PAGE, KV * HD)
    local_keys = slot_keys.reshape(slot_count * PAGE, KV * HD)
    local_values = slot_values.reshape(slot_count * PAGE, KV * HD)
    local_tokens = local_keys.shape[0]
    turned_q = rotate(
        queries.astype(jnp.float32).reshape(query_count, local_heads, HD), query_positions
    )
    own_queries = turned_q.astype(jnp.bfloat16).transpose(1, 0, 2)
    target = jnp.arange(devices, dtype=jnp.int32) * local_heads // per_group
    keys_by_head = local_keys.reshape(local_tokens, KV, HD).transpose(1, 0, 2)
    values_by_head = local_values.reshape(local_tokens, KV, HD).transpose(1, 0, 2)
    head_keys, head_values = (
        lax.all_to_all(keys_by_head[target], "ctx", split_axis=0, concat_axis=0, tiled=True),
        lax.all_to_all(values_by_head[target], "ctx", split_axis=0, concat_axis=0, tiled=True),
    )
    key_positions = (page_offsets[inverse][:, None] + in_page[None, :]).reshape(-1)
    key_live = (in_page[None, :] < page_lengths[inverse][:, None]).reshape(-1)
    key_positions, key_live = (key_positions, key_live)
    allowed = (key_positions[None, :] <= query_positions[:, None]) & key_live[None, :]
    span_devices = max(1, min(devices, 4096 // local_tokens))
    while span_devices > 1 and devices % span_devices:
        span_devices -= 1
    block_count = devices // span_devices
    key_blocks = head_keys.reshape(block_count, span_devices * local_tokens, HD)
    value_blocks = head_values.reshape(block_count, span_devices * local_tokens, HD)
    allowed_blocks = allowed.reshape(
        query_count, block_count, span_devices * local_tokens
    ).transpose(1, 0, 2)

    def block_scores(key_block, allow_block):
        scores = jnp.einsum(
            "hqd,kd->hqk", own_queries, key_block, preferred_element_type=jnp.float32
        ) * HD ** (-0.5)
        return jnp.where(allow_block[None], scores, masked_score)

    block_max = lax.map(
        lambda operands: jnp.max(block_scores(operands[0], operands[1]), axis=-1),
        (key_blocks, allowed_blocks),
    )
    row_max = jnp.max(block_max, axis=0)

    def weigh_block(operands):
        key_block, value_block, allow_block = operands
        weights = jnp.exp(block_scores(key_block, allow_block) - row_max[..., None])
        denominator = jnp.sum(weights, axis=-1)
        summed = jnp.einsum(
            "hqk,kd->hqd",
            weights.astype(jnp.bfloat16),
            value_block,
            preferred_element_type=jnp.float32,
        )
        return (summed, denominator)

    summed, denominator = lax.map(weigh_block, (key_blocks, value_blocks, allowed_blocks))
    summed = jnp.sum(summed, axis=0)
    denominator = jnp.sum(denominator, axis=0)
    attended = (summed / denominator[..., None]).astype(jnp.bfloat16)
    mixed = attended.transpose(1, 0, 2).reshape(query_count, local_heads * HD)
    reduced = lax.psum_scatter(
        lax.dot_general(
            out_weight, mixed, (((0,), (1,)), ((), ())), preferred_element_type=jnp.float32
        ),
        "ctx",
        scatter_dimension=0,
        tiled=True,
    )
    output = reduced.T.astype(jnp.bfloat16)
    return (new_keys, new_values, output)


def solution(mesh):
    in_specs = (
        P(("groups", "ctx"), None),
        P(("groups", "ctx"), None),
        P(("groups", "ctx"), None),
        P(("groups", "ctx"), None),
        P("groups"),
        P("groups"),
        P("groups"),
        P("groups"),
        P("groups", "ctx"),
        P("ctx", None),
    )
    out_specs = (P(("groups", "ctx"), None), P(("groups", "ctx"), None), P("groups", "ctx"))
    fits = mesh.shape["ctx"] == 2 * KV
    chosen = body if fits else wide_body
    return jax.shard_map(
        chosen, mesh=mesh, in_specs=in_specs, out_specs=out_specs, check_vma=False
    )
```

```python
import math

import jax
import jax.numpy as jnp
import numpy as np
from jax import lax
from jax.experimental import pallas as pl
from jax.experimental.pallas import tpu as pltpu
from jax.sharding import PartitionSpec as P


H = 128
KV = 8
HD = 128
PAGE = 16
MIB = 1 << 20
BLOCK = 512
HEADS_AT_ONCE = 2
EARLY = 8


rope_theta = 500000.0
scale_factor = 8.0
low_factor = 1.0
high_factor = 4.0
old_context = 8192.0
masked_score = -1e30
far_position = 1e9
VMEM = pl.BlockSpec(memory_space=pltpu.VMEM)
SMEM = pl.BlockSpec(memory_space=pltpu.SMEM)
HBM = pl.BlockSpec(memory_space=pltpu.HBM)
DMA = pltpu.SemaphoreType.DMA


def inverse_freq():
    exponent = np.arange(0, HD, 2).astype(np.float64) / HD
    base_freq = 1.0 / rope_theta**exponent
    wavelength = 2.0 * math.pi / base_freq
    smooth = (old_context / wavelength - low_factor) / (high_factor - low_factor)
    blended = (1.0 - smooth) * base_freq / scale_factor + smooth * base_freq
    short_wave = wavelength < old_context / high_factor
    longer = wavelength > old_context / low_factor
    return np.where(
        short_wave, base_freq, np.where(longer, base_freq / scale_factor, blended)
    ).astype(np.float32)


def lane_tables():
    freq = inverse_freq()
    sign = np.repeat([-1.0, 1.0], HD // 2)
    return jnp.asarray(np.stack([np.concatenate([freq, freq]), sign]).astype(np.float32))


def params(mib):
    return pltpu.CompilerParams(vmem_limit_bytes=mib * MIB)


def cost(flops, moved, exps=0):
    return pl.CostEstimate(flops=flops, bytes_accessed=moved, transcendentals=exps)


def shape(dims, dtype=jnp.bfloat16):
    return jax.ShapeDtypeStruct(dims, dtype)


def cos_sin(position, table_ref):
    angle = position * table_ref[0:1, :]
    return jnp.cos(angle), jnp.sin(angle) * table_ref[1:2, :]


def turn(x, cosine, sine):
    return x * cosine + pltpu.roll(x, HD // 2, 1) * sine


def column(row):
    n = row.shape[1]
    same = lax.broadcasted_iota(jnp.int32, (n, n), 0) == lax.broadcasted_iota(jnp.int32, (n, n), 1)
    return jnp.sum(jnp.where(same, row, 0.0), axis=1, keepdims=True)


def fetch(pairs, sems, meanwhile=None):
    copies = [pltpu.make_async_copy(a, b, sems.at[at]) for at, (a, b) in enumerate(pairs)]
    for copy in copies:
        copy.start()
    if meanwhile is not None:
        meanwhile()
    for copy in copies:
        copy.wait()


def in_hbm(xs):
    return [pltpu.with_memory_space_constraint(x, pltpu.HBM) for x in xs]


def vmem_like(x):
    return pltpu.VMEM(x.shape, x.dtype)


def rows_kernel(here_ref, *refs):
    inputs, out_refs, scratch, sems = refs[:8], refs[8:-9], refs[-9:-1], refs[-1]
    fetch(list(zip(inputs, scratch)), sems)
    ks_ref, vs_ref, table_ref, source_ref, lengths_ref, offsets_ref, pk_ref, pv_ref = scratch
    rows = pk_ref.shape[0]
    slots = rows // PAGE
    pages = source_ref.shape[1]
    row = lax.broadcasted_iota(jnp.int32, (rows, pages), 0)
    match = source_ref[...] == here_ref[0] * slots + row // PAGE

    def pick(ref):
        return jnp.sum(jnp.where(match, ref[...].astype(jnp.float32), 0.0), axis=1, keepdims=True)

    position, length = pick(offsets_ref), pick(lengths_ref)
    cosine, sine = cos_sin(position, table_ref)
    token = (lax.broadcasted_iota(jnp.int32, (rows, 1), 0) % PAGE).astype(jnp.float32)
    live = jnp.broadcast_to((token < length).astype(jnp.float32), (rows, HD))
    for piece, out_ref in enumerate(out_refs):
        head = jnp.bitwise_xor(here_ref[0] // 2, piece)
        lanes = pl.ds(pl.multiple_of(head * HD, HD), HD)
        for slot in range(slots):
            part = slice(slot * PAGE, (slot + 1) * PAGE)
            k = pk_ref[part, lanes].astype(jnp.float32) * ks_ref[slot, head]
            k = turn(k, cosine[part], sine[part]) * live[part]
            out_ref[0, part, :] = k.astype(jnp.bfloat16)
            v = pv_ref[part, lanes].astype(jnp.float32) * vs_ref[slot, head]
            out_ref[1, part, :] = (v * live[part]).astype(jnp.bfloat16)


def prepare_rows(here, pool_keys, pool_values, key_scales, value_scales, source, lengths, offsets):
    rows = pool_keys.shape[0]
    table = lane_tables()
    small = [pltpu.SMEM(key_scales.shape, jnp.float32)] * 2
    inputs = (key_scales, value_scales, table, source, lengths, offsets, pool_keys, pool_values)
    return pl.pallas_call(
        rows_kernel,
        out_shape=[shape((2, rows, HD))] * KV,
        in_specs=[SMEM] + [HBM] * 8,
        out_specs=[VMEM] * KV,
        scratch_shapes=small + [vmem_like(x) for x in inputs[2:]] + [DMA((8,))],
        name="prepare_rows",
        compiler_params=params(6),
        cost_estimate=cost(20 * rows * KV * HD, 8 * rows * KV * HD),
    )(here, *in_hbm(inputs))


def weight_parts(w_ref, pieces, refs, count):
    parts = []
    for (first, last), ref in zip(pieces, refs):
        rows = (last - first) // count
        for at in range(count):
            parts.append(
                (
                    w_ref.at[first + at * rows : first + (at + 1) * rows, :],
                    ref.at[at * rows : (at + 1) * rows, :],
                )
            )
    return parts


def weight_shapes(pieces, out_weight):
    return [shape((last - first, out_weight.shape[1])) for first, last in pieces]


def side_kernel(pieces, owners, here_ref, w_ref, *refs):
    inputs, outs, refs = refs[:6], refs[6:8], refs[8:]
    held, scratch, sems, weight_sems = refs[: len(pieces)], refs[len(pieces) : -2], refs[-2], refs[-1]

    def compute():
        fetch(list(zip(inputs, scratch)), sems)
        side_rows(here_ref, *scratch, *outs)

    fetch(weight_parts(w_ref, pieces, held, owners), weight_sems, compute)


def side_rows(here_ref, *refs):
    (out_ref, kpos_ref), scratch = refs[-2:], refs[:-2]
    table_ref, source_ref, lengths_ref, offsets_ref, position_ref, q_ref = scratch
    count = q_ref.shape[0]
    cosine, sine = cos_sin(column(position_ref[...].astype(jnp.float32)), table_ref)
    for head in range(q_ref.shape[1] // HD):
        q = q_ref[:, head * HD : (head + 1) * HD].astype(jnp.float32)
        out_ref[head * count : (head + 1) * count, :] = turn(q, cosine, sine).astype(jnp.bfloat16)
    source = column(source_ref[...].astype(jnp.float32))
    length = column(lengths_ref[...].astype(jnp.float32))
    offset = column(offsets_ref[...].astype(jnp.float32))
    tokens = kpos_ref.shape[1]
    rows = tokens // (2 * KV)
    slots = rows // PAGE
    at = lax.broadcasted_iota(jnp.int32, (1, rows), 1)
    token = (at % PAGE).astype(jnp.float32)
    where = jnp.where(token < length, offset + token, far_position)
    for group in range(2 * KV):
        half, piece = group // KV, group % KV
        device = jnp.bitwise_xor(here_ref[0], 2 * piece + half)
        page = (device * slots + at // PAGE).astype(jnp.float32)
        kpos_ref[:, group * rows : (group + 1) * rows] = jnp.sum(
            jnp.where(source == page, where, 0.0), axis=0, keepdims=True
        )


def side(here, source, lengths, offsets, positions, queries, out_weight, pieces, owners):
    count, width = queries.shape
    tokens = source.shape[1] * PAGE
    inputs = (lane_tables(), source, lengths, offsets, positions, queries)
    outs = [shape((count * (width // HD), HD)), shape((1, tokens), jnp.float32)]
    outs += weight_shapes(pieces, out_weight)
    return pl.pallas_call(
        lambda *refs: side_kernel(pieces, owners, *refs),
        out_shape=outs,
        in_specs=[SMEM] + [HBM] * 7,
        out_specs=[VMEM] * len(outs),
        scratch_shapes=[vmem_like(x) for x in inputs] + [DMA((6,)), DMA((len(pieces) * owners,))],
        name="side",
        compiler_params=params(6),
        cost_estimate=cost(8 * count * width, 64 * MIB),
    )(here, *in_hbm((out_weight, *inputs)))


def assemble_kernel(*refs):
    for at, ref in enumerate(refs[:-1]):
        refs[-1][at] = ref[...]


def assemble(pieces):
    dims = (len(pieces), *pieces[0].shape)
    return pl.pallas_call(
        assemble_kernel,
        out_shape=shape(dims),
        in_specs=[VMEM] * len(pieces),
        out_specs=VMEM,
        compiler_params=params(2),
        cost_estimate=cost(0, 4 * math.prod(dims)),
    )(*pieces)


def pages_kernel(here_ref, source_ref, *refs):
    *context, near_ref, far_ref, page_ref, place_ref = refs
    pages = source_ref.shape[0]
    slots = pages // (2 * KV)
    here = here_ref[0]
    kind = here % 2
    for page in range(pages):
        place_ref[source_ref[page]] = page
    group = 0
    for ref in context:
        for at in range(ref.shape[0]):
            half, piece = group // KV, group % KV
            device = jnp.bitwise_xor(here, 2 * piece + half)
            for slot in range(slots):
                page = place_ref[device * slots + slot]
                page_ref[page] = ref[at, kind, slot * PAGE : (slot + 1) * PAGE, :]
            group += 1
    for piece in range(KV):
        first = jnp.bitwise_xor(here // 2, piece) * 2 * slots
        out_ref = near_ref if piece < KV // 2 else far_ref
        out_ref[piece % (KV // 2)] = page_ref[pl.ds(first, 2 * slots)]


def order_pages(here, source, context):
    pages = source.shape[0]
    return pl.pallas_call(
        pages_kernel,
        out_shape=[shape((KV // 2, pages // KV, PAGE, HD))] * 2,
        in_specs=[SMEM, SMEM] + [VMEM] * len(context),
        out_specs=[VMEM] * 2,
        scratch_shapes=[pltpu.VMEM((pages, PAGE, HD), jnp.bfloat16), pltpu.SMEM((pages,), jnp.int32)],
        name="order_pages",
        compiler_params=params(4),
        cost_estimate=cost(0, 4 * pages * PAGE * HD),
    )(here, source, *context)


def forward_kernel(first, *refs):
    *held, out_ref = refs
    at = 0
    for ref in held:
        for row in range(ref.shape[0]):
            out_ref[at] = ref[row, first : first + out_ref.shape[1]]
            at += 1


def forward(held, first):
    count = sum(x.shape[0] for x in held)
    dims = (count, first, *held[0].shape[2:])
    return pl.pallas_call(
        lambda *refs: forward_kernel(first, *refs),
        out_shape=shape(dims),
        in_specs=[VMEM] * len(held),
        out_specs=VMEM,
        compiler_params=params(4),
        cost_estimate=cost(0, 4 * math.prod(dims)),
    )(*held)


def send_pages(near, far, devices):
    held, heads = [near[None]], [0]
    send = far[None]
    bit = KV // 2
    while True:
        held.append(swap(send, 2 * bit, devices))
        heads += [head | bit for head in heads]
        bit //= 2
        if not bit:
            break
        send = forward(held, bit)
    return held, heads


def collect_kernel(heads, here_ref, *refs):
    *held, keep_ref, send_ref = refs
    rows = keep_ref.shape[0]
    slots = rows // PAGE
    core = here_ref[0] % 2
    pieces = [(ref, row) for ref in held for row in range(ref.shape[0])]
    for (ref, row), apart in zip(pieces, heads):
        head = jnp.bitwise_xor(here_ref[0] // 2, apart)
        lanes = pl.ds(pl.multiple_of(head * HD, HD), HD)
        keep_ref[:, lanes] = ref[row, 0, pl.ds(core * slots, slots)].reshape(rows, HD)
        send_ref[:, lanes] = ref[row, 0, pl.ds((1 - core) * slots, slots)].reshape(rows, HD)


def collect_heads(here, held, heads):
    rows = held[0].shape[2] * PAGE // 2
    out = shape((rows, KV * HD))
    return pl.pallas_call(
        lambda *refs: collect_kernel(heads, *refs),
        out_shape=(out, out),
        in_specs=[SMEM] + [VMEM] * len(held),
        out_specs=(VMEM, VMEM),
        name="collect_heads",
        compiler_params=params(4),
        cost_estimate=cost(0, 8 * rows * KV * HD),
    )(here, *held)


def settle_kernel(here_ref, mine_ref, other_ref, keys_ref, values_ref):
    first = here_ref[0] % 2 == 0
    keys_ref[...] = jnp.where(first, mine_ref[...], other_ref[...])
    values_ref[...] = jnp.where(first, other_ref[...], mine_ref[...])


def settle(here, mine, other):
    return pl.pallas_call(
        settle_kernel,
        out_shape=(shape(mine.shape), shape(mine.shape)),
        in_specs=[SMEM, VMEM, VMEM],
        out_specs=(VMEM, VMEM),
        name="settle",
        compiler_params=params(4),
        cost_estimate=cost(0, 8 * math.prod(mine.shape)),
    )(here, mine, other)


def attention_kernel(pieces, owners, w_ref, *refs):
    s_ref, sems = refs[-2:]
    held = refs[-2 - len(pieces) : -2]
    *refs, out_ref = refs[: -2 - len(pieces)]
    parts = weight_parts(w_ref, pieces, held, owners)
    fetch(parts, sems, lambda: attention_heads(*refs, out_ref, s_ref))


def attention_heads(*refs):
    context, (q_ref, kpos_ref, qpos_ref, out_ref, s_ref) = refs[:-5], refs[-5:]
    count = qpos_ref.shape[1]
    heads = q_ref.shape[0] // count
    group = s_ref.shape[0] // count
    rows = context[0].shape[2]
    blocks, at = [], 0
    for ref in context:
        step = max(1, min(ref.shape[0], BLOCK // rows))
        for first in range(0, ref.shape[0], step):
            blocks.append((ref, slice(first, first + step), slice(at, at + step * rows)))
            at += step * rows
    block = step * rows
    scale = HD**-0.5 * math.log2(math.e)
    qpos = column(qpos_ref[...].astype(jnp.float32))
    qpos = jnp.concatenate([qpos] * group, axis=0)
    size = group * count

    def one(index, carry):
        q = q_ref[pl.ds(pl.multiple_of(index * size, size), size), :]
        top = jnp.full((size, HD), masked_score, jnp.float32)
        for ref, chips, lanes in blocks:
            s = lax.dot_general(
                q,
                ref[chips, 0].reshape(block, HD),
                (((1,), (1,)), ((), ())),
                preferred_element_type=jnp.float32,
            )
            s = jnp.where(kpos_ref[:, lanes] <= qpos, s, masked_score)
            s_ref[:, lanes] = s
            for lane in range(0, block, HD):
                top = jnp.maximum(top, s[:, lane : lane + HD])
        top = jnp.max(top, axis=1, keepdims=True)
        total = jnp.zeros((size, HD), jnp.float32)
        summed = jnp.zeros((size, HD), jnp.float32)
        for ref, chips, lanes in blocks:
            w = jnp.exp2((s_ref[:, lanes] - top) * scale)
            for lane in range(0, block, HD):
                total = total + w[:, lane : lane + HD]
            summed = summed + jnp.dot(
                w.astype(jnp.bfloat16),
                ref[chips, 1].reshape(block, HD),
                preferred_element_type=jnp.float32,
            )
        out = (summed / jnp.sum(total, axis=1, keepdims=True)).astype(jnp.bfloat16)
        for at in range(group):
            lanes = pl.ds(pl.multiple_of((index * group + at) * HD, HD), HD)
            out_ref[:, lanes] = out[at * count : (at + 1) * count]
        return carry

    lax.fori_loop(0, heads // group, one, 0, unroll=2)


def attend(context, q, key_positions, query_positions, out_weight, pieces, owners):
    tokens = key_positions.shape[1]
    count = query_positions.shape[1]
    heads = q.shape[0] // count
    outs = [shape((count, heads * HD))] + weight_shapes(pieces, out_weight)
    return pl.pallas_call(
        lambda *refs: attention_kernel(pieces, owners, *refs),
        out_shape=outs,
        in_specs=[HBM] + [VMEM] * (len(context) + 3),
        out_specs=[VMEM] * len(outs),
        scratch_shapes=[
            pltpu.VMEM((math.gcd(heads, HEADS_AT_ONCE) * count, tokens), jnp.float32),
            DMA((len(pieces) * owners,)),
        ],
        name="attend",
        compiler_params=params(8),
        cost_estimate=cost(
            4 * count * heads * tokens * HD, 4 * tokens * HD, count * heads * tokens
        ),
    )(*in_hbm([out_weight]), *context, q, key_positions, query_positions)


def fold_masks(bits):
    masks = [0]
    for bit in reversed(bits):
        masks = masks + [m | bit for m in masks]
    return masks


def columns_of(here_ref, mask, start, width, w_ref):
    own_width = w_ref.shape[1] // (2 * KV)
    first = jnp.bitwise_xor(here_ref[0], mask) * own_width + start
    return pl.ds(pl.multiple_of(first, HD), width)


def product(x_ref, w_refs, columns):
    total, first = None, 0
    for ref in w_refs:
        last = first + ref.shape[0]
        y = jnp.dot(x_ref[:, first:last], ref[:, columns], preferred_element_type=jnp.float32)
        total = y if total is None else total + y
        first = last
    return total


def project_send_kernel(masks, start, here_ref, x_ref, *refs):
    *w_refs, out_ref = refs
    for at, mask in enumerate(masks):
        columns = columns_of(here_ref, mask, start, out_ref.shape[2], w_refs[0])
        out_ref[at] = product(x_ref, w_refs, columns).astype(jnp.bfloat16)


def project_add_kernel(masks, start, first, here_ref, x_ref, *refs):
    *w_refs, got_ref, out_ref = refs
    for at, mask in enumerate(masks):
        columns = columns_of(here_ref, mask, start, got_ref.shape[2], w_refs[0])
        y = product(x_ref, w_refs, columns) + got_ref[first + at].astype(jnp.float32)
        out_ref[at] = y.astype(out_ref.dtype)


def project_cost(x, columns):
    return cost(2 * x.shape[0] * x.shape[1] * columns, 2 * x.shape[1] * columns)


def project_send(here, mixed, weights, masks, start, width):
    count = mixed.shape[0]
    return pl.pallas_call(
        lambda *refs: project_send_kernel(masks, start, *refs),
        out_shape=shape((len(masks), count, width)),
        in_specs=[SMEM, VMEM] + [VMEM] * len(weights),
        out_specs=VMEM,
        compiler_params=params(6),
        cost_estimate=project_cost(mixed, len(masks) * width),
    )(here, mixed, *weights)


def project_add(here, mixed, weights, got, masks, start, first, dtype):
    count = mixed.shape[0]
    width = got.shape[2]
    return pl.pallas_call(
        lambda *refs: project_add_kernel(masks, start, first, *refs),
        out_shape=shape((len(masks), count, width), dtype),
        in_specs=[SMEM, VMEM] + [VMEM] * len(weights) + [VMEM],
        out_specs=VMEM,
        compiler_params=params(6),
        cost_estimate=project_cost(mixed, len(masks) * width),
    )(here, mixed, *weights, got)


def fold_kernel(keep_ref, got_ref, send_ref, left_ref):
    left = left_ref.shape[0]
    for at in range(left):
        send_ref[at] = (keep_ref[left + at] + got_ref[left + at].astype(jnp.float32)).astype(
            jnp.bfloat16
        )
    for at in range(left):
        left_ref[at] = keep_ref[at] + got_ref[at].astype(jnp.float32)


def fold(keep, got):
    owners, count, width = keep.shape
    half = (owners // 2, count, width)
    return pl.pallas_call(
        fold_kernel,
        out_shape=(shape(half), shape(half, jnp.float32)),
        in_specs=[VMEM, VMEM],
        out_specs=(VMEM, VMEM),
        compiler_params=params(4),
        cost_estimate=cost(owners * count * width, 8 * owners * count * width),
    )(keep, got)


def finish_kernel(*refs):
    out_ref, at = refs[-1], 0
    for keep_ref, got_ref in zip(refs[:-1:2], refs[1:-1:2]):
        width = keep_ref.shape[2]
        total = keep_ref[0] + got_ref[0].astype(jnp.float32)
        out_ref[:, at : at + width] = total.astype(jnp.bfloat16)
        at += width


def finish(pairs):
    flat = [x for pair in pairs for x in pair]
    count = flat[0].shape[1]
    width = sum(keep.shape[2] for keep, _ in pairs)
    return pl.pallas_call(
        finish_kernel,
        out_shape=shape((count, width)),
        in_specs=[VMEM] * len(flat),
        out_specs=VMEM,
        name="finish",
        compiler_params=params(4),
        cost_estimate=cost(count * width, 8 * count * width),
    )(*flat)


def swap(x, bits, devices):
    return lax.ppermute(x, "ctx", [(d, d ^ bits) for d in range(devices)])


def after(x, *others):
    return lax.optimization_barrier((x, *others))[0]


def plan(devices, own_width):
    bits = [1 << b for b in range(devices.bit_length() - 1)]
    half, quarter = own_width // 2, own_width // 4
    swapped = [bits[0], bits[2], bits[1]] + bits[3:]
    return [(0, half, bits), (half, quarter, swapped), (half + quarter, quarter, bits)]


def project_and_scatter(here, devices, x, weights, chunks):
    masks = [fold_masks(order) for _, _, order in chunks]
    half, quarter = devices // 2, devices // 4
    got, sends, keeps = [], [], []
    for at, (start, width, order) in enumerate(chunks):
        out = project_send(here, x, weights, masks[at][half:], start, width)
        got.append(swap(out, order[0], devices))
        x = after(x, out)
    for dtype, into, first in ((jnp.bfloat16, sends, quarter), (jnp.float32, keeps, 0)):
        for at, (start, _, _) in enumerate(chunks):
            part = masks[at][first : first + quarter]
            y = project_add(here, x, weights, got[at], part, start, first, dtype)
            into.append(y)
            x = after(x, y)
    state = list(zip(sends, keeps))
    stages = len(chunks[0][2])
    for stage in range(1, stages):
        arrived = [swap(send, chunks[at][2][stage], devices) for at, (send, _) in enumerate(state)]
        if stage + 1 < stages:
            state = [fold(keep, got) for (_, keep), got in zip(state, arrived)]
    return finish([(keep, got) for (_, keep), got in zip(state, arrived)])


def body(
    pool_keys,
    pool_values,
    key_scales,
    value_scales,
    page_source,
    page_lengths,
    page_offsets,
    query_positions,
    queries,
    out_weight,
):
    devices = lax.axis_size("ctx")
    here = lax.axis_index("ctx").astype(jnp.int32)[None]
    source, lengths, offsets = page_source[None], page_lengths[None], page_offsets[None]
    positions = query_positions[None]
    depth = out_weight.shape[0]
    chunks = plan(devices, out_weight.shape[1] // devices)
    early = depth * EARLY // 16
    pieces = prepare_rows(
        here, pool_keys, pool_values, key_scales, value_scales, source, lengths, offsets
    )
    far = range(KV // 2, KV)
    arrived = [pieces[0]] + [swap(pieces[k], 2 * k, devices) for k in range(1, KV)]
    turned, key_positions, *side_weights = side(
        here, source, lengths, offsets, positions, queries, out_weight, [(0, early)], 8
    )
    near = assemble(arrived[: KV // 2])
    far = assemble(arrived[KV // 2 :])
    context = [near, far, swap(near, 1, devices), swap(far, 1, devices)]
    near_pages, far_pages = order_pages(here, page_source, context)
    held, heads = send_pages(near_pages, far_pages, devices)
    mixed, *late_weights = attend(
        context, turned, key_positions, positions, out_weight, [(early, depth)], 8
    )
    weights = [*side_weights, *late_weights]
    output = project_and_scatter(here, devices, mixed, weights, chunks)
    mine, partner = collect_heads(here, held, heads)
    new_keys, new_values = settle(here, mine, swap(partner, 1, devices))
    return (new_keys, new_values, output)


def wide_inverse_freq():
    exponent = jnp.arange(0, HD, 2).astype(jnp.float32) / HD
    base_freq = 1.0 / rope_theta**exponent
    wavelength = 2.0 * math.pi / base_freq
    smooth = (old_context / wavelength - low_factor) / (high_factor - low_factor)
    blended = (1.0 - smooth) * base_freq / scale_factor + smooth * base_freq
    short_wave = wavelength < old_context / high_factor
    longer = wavelength > old_context / low_factor
    return jnp.where(short_wave, base_freq, jnp.where(longer, base_freq / scale_factor, blended))


def rotate(values, positions):
    angle = positions.astype(jnp.float32)[:, None] * wide_inverse_freq()[None, :]
    cosine = jnp.cos(angle)[:, None, :]
    sine_part = jnp.sin(angle)[:, None, :]
    half_size = values.shape[-1] // 2
    first_half = values[..., :half_size]
    second = values[..., half_size:]
    return jnp.concatenate(
        [first_half * cosine - second * sine_part, second * cosine + first_half * sine_part],
        axis=-1,
    )


def wide_body(
    pool_keys,
    pool_values,
    key_scales,
    value_scales,
    page_source,
    page_lengths,
    page_offsets,
    query_positions,
    queries,
    out_weight,
):
    devices = lax.axis_size("ctx")
    here_index = lax.axis_index("ctx")
    slot_count = key_scales.shape[0]
    page_count = page_source.shape[0]
    query_count = queries.shape[0]
    local_heads = queries.shape[1] // HD
    per_group = H // KV
    in_page = jnp.arange(PAGE, dtype=jnp.int32)
    inverse = (
        jnp.zeros((page_count,), jnp.int32)
        .at[page_source]
        .set(jnp.arange(page_count, dtype=jnp.int32))
    )
    held_pages = lax.dynamic_slice_in_dim(inverse, here_index * slot_count, slot_count)
    held_live = in_page[None, :] < page_lengths[held_pages][:, None]
    live_float = held_live.reshape(-1).astype(jnp.float32)[:, None, None]
    scaled_keys = (
        pool_keys.reshape(slot_count, PAGE, KV, HD).astype(jnp.float32)
        * key_scales[:, None, :, None]
    )
    scaled_values = (
        pool_values.reshape(slot_count, PAGE, KV, HD).astype(jnp.float32)
        * value_scales[:, None, :, None]
    )
    turned = rotate(
        scaled_keys.reshape(slot_count * PAGE, KV, HD), jnp.repeat(page_offsets[held_pages], PAGE)
    )
    slot_keys = (turned * live_float).astype(jnp.bfloat16).reshape(slot_count, PAGE * KV * HD)
    slot_values = (
        (scaled_values.reshape(slot_count * PAGE, KV, HD) * live_float)
        .astype(jnp.bfloat16)
        .reshape(slot_count, PAGE * KV * HD)
    )
    owner_device = held_pages // slot_count
    routing = (owner_device[None, :] == jnp.arange(devices, dtype=jnp.int32)[:, None]).astype(
        jnp.bfloat16
    )
    outgoing_keys = jnp.dot(routing, slot_keys, preferred_element_type=jnp.float32).astype(
        jnp.bfloat16
    )
    outgoing_values = jnp.dot(routing, slot_values, preferred_element_type=jnp.float32).astype(
        jnp.bfloat16
    )
    arrived_keys, arrived_values = (
        lax.all_to_all(outgoing_keys, "ctx", split_axis=0, concat_axis=0, tiled=True),
        lax.all_to_all(outgoing_values, "ctx", split_axis=0, concat_axis=0, tiled=True),
    )
    assembled_pages = here_index * slot_count + jnp.arange(slot_count, dtype=jnp.int32)
    sender = page_source[assembled_pages] // slot_count
    new_keys = arrived_keys[sender].reshape(slot_count * PAGE, KV * HD)
    new_values = arrived_values[sender].reshape(slot_count * PAGE, KV * HD)
    local_keys = slot_keys.reshape(slot_count * PAGE, KV * HD)
    local_values = slot_values.reshape(slot_count * PAGE, KV * HD)
    local_tokens = local_keys.shape[0]
    turned_q = rotate(
        queries.astype(jnp.float32).reshape(query_count, local_heads, HD), query_positions
    )
    own_queries = turned_q.astype(jnp.bfloat16).transpose(1, 0, 2)
    target = jnp.arange(devices, dtype=jnp.int32) * local_heads // per_group
    keys_by_head = local_keys.reshape(local_tokens, KV, HD).transpose(1, 0, 2)
    values_by_head = local_values.reshape(local_tokens, KV, HD).transpose(1, 0, 2)
    head_keys, head_values = (
        lax.all_to_all(keys_by_head[target], "ctx", split_axis=0, concat_axis=0, tiled=True),
        lax.all_to_all(values_by_head[target], "ctx", split_axis=0, concat_axis=0, tiled=True),
    )
    key_positions = (page_offsets[inverse][:, None] + in_page[None, :]).reshape(-1)
    key_live = (in_page[None, :] < page_lengths[inverse][:, None]).reshape(-1)
    key_positions, key_live = (key_positions, key_live)
    allowed = (key_positions[None, :] <= query_positions[:, None]) & key_live[None, :]
    span_devices = max(1, min(devices, 4096 // local_tokens))
    while span_devices > 1 and devices % span_devices:
        span_devices -= 1
    block_count = devices // span_devices
    key_blocks = head_keys.reshape(block_count, span_devices * local_tokens, HD)
    value_blocks = head_values.reshape(block_count, span_devices * local_tokens, HD)
    allowed_blocks = allowed.reshape(
        query_count, block_count, span_devices * local_tokens
    ).transpose(1, 0, 2)

    def block_scores(key_block, allow_block):
        scores = jnp.einsum(
            "hqd,kd->hqk", own_queries, key_block, preferred_element_type=jnp.float32
        ) * HD ** (-0.5)
        return jnp.where(allow_block[None], scores, masked_score)

    block_max = lax.map(
        lambda operands: jnp.max(block_scores(operands[0], operands[1]), axis=-1),
        (key_blocks, allowed_blocks),
    )
    row_max = jnp.max(block_max, axis=0)

    def weigh_block(operands):
        key_block, value_block, allow_block = operands
        weights = jnp.exp(block_scores(key_block, allow_block) - row_max[..., None])
        denominator = jnp.sum(weights, axis=-1)
        summed = jnp.einsum(
            "hqk,kd->hqd",
            weights.astype(jnp.bfloat16),
            value_block,
            preferred_element_type=jnp.float32,
        )
        return (summed, denominator)

    summed, denominator = lax.map(weigh_block, (key_blocks, value_blocks, allowed_blocks))
    summed = jnp.sum(summed, axis=0)
    denominator = jnp.sum(denominator, axis=0)
    attended = (summed / denominator[..., None]).astype(jnp.bfloat16)
    mixed = attended.transpose(1, 0, 2).reshape(query_count, local_heads * HD)
    reduced = lax.psum_scatter(
        lax.dot_general(
            out_weight, mixed, (((0,), (1,)), ((), ())), preferred_element_type=jnp.float32
        ),
        "ctx",
        scatter_dimension=0,
        tiled=True,
    )
    output = reduced.T.astype(jnp.bfloat16)
    return (new_keys, new_values, output)


def solution(mesh):
    in_specs = (
        P(("groups", "ctx"), None),
        P(("groups", "ctx"), None),
        P(("groups", "ctx"), None),
        P(("groups", "ctx"), None),
        P("groups"),
        P("groups"),
        P("groups"),
        P("groups"),
        P("groups", "ctx"),
        P("ctx", None),
    )
    out_specs = (P(("groups", "ctx"), None), P(("groups", "ctx"), None), P("groups", "ctx"))
    fits = mesh.shape["ctx"] == 2 * KV
    chosen = body if fits else wide_body
    return jax.shard_map(
        chosen, mesh=mesh, in_specs=in_specs, out_specs=out_specs, check_vma=False
    )
```
